32 devices in a mesh: body: 4 (over y, core), surf: 8 (over z, x).
Axes of the slice: x: 2, y: 2, z: 4, core: 2. Of those that a mesh axis runs over, the one named last changes fastest.
Arguments:
- external_load: float32 [3, 32, 128, 1024], P(None, 'body', 'surf'), may hold values from -18 to 18
- modulus: float32 [32, 128, 1024], P('body', 'surf'), may hold values from 0.2 to 10, as said below
- active: int32 [128, 1024], P('surf'), may hold values 0 or 1
Outputs:
- lam_depth: float32 [3, 4, 128, 1024], P(None, 'body', 'surf')
- lam_surface: float32 [3, 32, 8, 1024], P(None, 'body', 'surf')
- lam_contact: float32 [4, 128, 1024], P('body', 'surf')
The draws below stay inside these ranges and needn't reach their ends.
Inputs may be any that keep to these rules, and one draw needn't show every extreme that they name: The modulus is positive.
All inputs are finite; a program needn't handle non-finite values. No bound on the sum of `active` on one device may be relied on, other than what follows from the above.
Results may differ from the reference program's by a relative error of at most 0.0003.
Values sent between devices are 32-bit elements; how exact they have to be, the bound alone decides.
A program may use at most 192 MiB of HBM per device.

```python
import math
import jax
import jax.numpy as jnp
from jax import lax

SX = 8
SY = 16
SZ = 1024
ITERS = 3
SWEEPS = 6
NX = 32
NY = 128
N_BODY = 4
N_SURF = 8


def draw_external_load(key, part):
    rough_key = jax.random.fold_in(jax.random.fold_in(key, 11), 0)
    depth_rise = (jnp.arange(NX, dtype=jnp.float32) / NX)[None, :, None, None]
    across_rise = (jnp.arange(NY, dtype=jnp.float32) / NY)[None, None, :, None]
    scale_field = 0.5 * (1.0 + 2.0 * depth_rise) * (1.0 + 2.0 * across_rise)
    rough = jnp.clip(jax.random.normal(rough_key, (3, NX, NY, SZ), jnp.float32), -4.0, 4.0)
    return rough * scale_field


def draw_modulus(key, part):
    layer_key, node_key = jax.random.split(jax.random.fold_in(key, 23))
    layers = jnp.exp(jax.random.uniform(layer_key, (NX, 1, 1), jnp.float32, math.log(0.5), math.log(4.0)))
    nodes = jnp.exp(jax.random.uniform(node_key, (NX, NY, SZ), jnp.float32, math.log(0.4), math.log(2.5)))
    return layers * nodes


def place_ends(entries, stream_key, smallest, top_value):
    place = [jax.random.randint(jax.random.fold_in(stream_key, axis), (), 0, length) for axis, length in enumerate(entries.shape)]
    widest = entries.shape.index(max(entries.shape))
    next_to = place[:widest] + [(place[widest] + 1) % entries.shape[widest]] + place[widest + 1:]
    return entries.at[tuple(place)].set(smallest).at[tuple(next_to)].set(top_value)


def setup_inputs(seed: int = 0) -> dict:
    seeds = jax.random.split(jax.random.key(seed), 4)
    external_load = draw_external_load(jax.random.fold_in(seeds[3], 71), 0)
    modulus = draw_modulus(jax.random.fold_in(seeds[3], 71), 0)
    active = place_ends((jax.random.randint(seeds[2], (NY, SZ), 0, 2) < 1).astype(jnp.int32), jax.random.fold_in(seeds[2], 1), 0, 1)
    return {"external_load": external_load, "modulus": modulus, "active": active}


OFFSETS = [(plane_x, plane_y, plane_z) for plane_x in (-1, 0, 1) for plane_y in (-1, 0, 1) for plane_z in (-1, 0, 1) if (plane_x, plane_y, plane_z) != (0, 0, 0)]
COUPLING_SCALE = (0.0, 1.0, 0.5, 0.25)
RELAXATION = 0.6

def coupling(modulus, padded, offset):
    cells_x, cells_y, cells_z = modulus.shape
    nearby = padded[1 + offset[0]:1 + offset[0] + cells_x, 1 + offset[1]:1 + offset[1] + cells_y, 1 + offset[2]:1 + offset[2] + cells_z]
    weight = COUPLING_SCALE[abs(offset[0]) + abs(offset[1]) + abs(offset[2])]
    return weight * 2.0 * modulus * nearby / (modulus + nearby)

def inexact_solve(source, modulus):
    cells_x, cells_y, cells_z = modulus.shape
    padded = jnp.pad(modulus, 1)
    weights = [coupling(modulus, padded, offset) for offset in OFFSETS]
    diagonal = jnp.zeros_like(modulus)
    for weight_field in weights:
        diagonal = diagonal + weight_field
    iterate = RELAXATION * source / diagonal
    for repeat in range(SWEEPS - 1):
        spread = jnp.pad(iterate, ((0, 0), (1, 1), (1, 1), (1, 1)))
        applied = diagonal * iterate
        for offset, weight_field in zip(OFFSETS, weights):
            neighbour = spread[:, 1 + offset[0]:1 + offset[0] + cells_x, 1 + offset[1]:1 + offset[1] + cells_y, 1 + offset[2]:1 + offset[2] + cells_z]
            applied = applied - weight_field * neighbour
        iterate = iterate + RELAXATION * (source - applied) / diagonal
    return iterate

def coarse_factors(counts, n_depth, n_across, face_x, face_y):
    eye_depth = jnp.eye(n_depth, dtype=jnp.float32)
    path_matrix = 2.0 * eye_depth - jnp.eye(n_depth, k=1, dtype=jnp.float32) - jnp.eye(n_depth, k=-1, dtype=jnp.float32)
    path_matrix = path_matrix.at[0, 0].set(1.0)
    eye_across = jnp.eye(n_across, dtype=jnp.float32)
    cycle_matrix = 2.0 * eye_across - jnp.roll(eye_across, 1, axis=1) - jnp.roll(eye_across, -1, axis=1)
    base_matrix = face_x * jnp.kron(path_matrix, eye_across) + face_y * jnp.kron(eye_depth, cycle_matrix)
    normal_factor = jnp.linalg.cholesky(base_matrix + jnp.diag(counts))
    tangent_factor = jnp.linalg.cholesky(base_matrix)
    return (normal_factor, tangent_factor)

def coarse_solve(normal_factor, tangent_factor, coarse_rhs):
    normal_part = jax.scipy.linalg.cho_solve((normal_factor, True), coarse_rhs[0])
    tangent_part = jax.scipy.linalg.cho_solve((tangent_factor, True), coarse_rhs[1:].T).T
    return jnp.concatenate([normal_part[None], tangent_part], 0)

def transpose_apply(upper, lower, right_face, left_face, contact, mask_face, cells_x, cells_y):
    field = jnp.zeros((3, cells_x, cells_y, upper.shape[-1]), jnp.float32)
    field = field.at[:, cells_x - 1].add(upper)
    field = field.at[:, 0].add(-lower)
    field = field.at[:, :, cells_y - 1].add(right_face)
    field = field.at[:, :, 0].add(-left_face)
    field = field.at[0, 0].add(-contact * mask_face)
    return field

def reference(external_load, modulus, active):
    n_depth, n_across = (N_BODY, N_SURF)
    count_sub = n_depth * n_across
    load_blocks = external_load.reshape(3, n_depth, SX, n_across, SY, SZ).transpose(1, 3, 0, 2, 4, 5).reshape(count_sub, 3, SX, SY, SZ)
    modulus_blocks = modulus.reshape(n_depth, SX, n_across, SY, SZ).transpose(0, 2, 1, 3, 4).reshape(count_sub, SX, SY, SZ)
    mask_full = jnp.zeros((n_depth, n_across, SY, SZ), jnp.float32).at[0].set(active.astype(jnp.float32).reshape(n_across, SY, SZ))
    counts = jnp.sum(mask_full, axis=(2, 3)).reshape(count_sub)
    normal_factor, tangent_factor = coarse_factors(counts, n_depth, n_across, float(SY * SZ), float(SX * SZ))

    def lift(coarse_alpha):
        grid_alpha = coarse_alpha.reshape(3, n_depth, n_across).transpose(1, 2, 0)
        above = jnp.concatenate([grid_alpha[1:], jnp.zeros_like(grid_alpha[:1])], 0)
        right_alpha = jnp.roll(grid_alpha, -1, axis=1)
        depth_rows = jnp.broadcast_to((grid_alpha - above)[:, :, :, None, None], (n_depth, n_across, 3, SY, SZ))
        across_rows = jnp.broadcast_to((grid_alpha - right_alpha)[:, :, :, None, None], (n_depth, n_across, 3, SX, SZ))
        contact_rows = -grid_alpha[:, :, 0][:, :, None, None] * mask_full
        return (depth_rows, across_rows, contact_rows)

    def restrict(vector):
        sums_x = jnp.sum(vector[0], axis=(3, 4))
        sums_y = jnp.sum(vector[1], axis=(3, 4))
        sums_c = jnp.sum(vector[2], axis=(2, 3))
        below = jnp.concatenate([jnp.zeros_like(sums_x[:1]), sums_x[:-1]], 0)
        totals = sums_x - below + sums_y - jnp.roll(sums_y, 1, axis=1)
        totals = totals.at[:, :, 0].add(-sums_c)
        return totals.transpose(2, 0, 1).reshape(3, count_sub)

    def inner(first, second):
        return jnp.sum(first[0] * second[0]) + jnp.sum(first[1] * second[1]) + jnp.sum(first[2] * second[2])

    def combine(first, second, factor):
        return tuple((left_part + factor * right_part for left_part, right_part in zip(first, second)))

    def project(vector):
        coarse_alpha = coarse_solve(normal_factor, tangent_factor, restrict(vector))
        return combine(vector, lift(coarse_alpha), -1.0)

    def traces(vector, with_load):
        lower = jnp.concatenate([jnp.zeros_like(vector[0][:1]), vector[0][:-1]], 0)
        left_rows = jnp.roll(vector[1], 1, axis=1)
        pieces = (vector[0], lower, vector[1], left_rows, vector[2], mask_full)
        flat = tuple((piece.reshape((count_sub,) + piece.shape[2:]) for piece in pieces)) + (modulus_blocks, load_blocks)

        def one_block(items):
            field = transpose_apply(items[0], items[1], items[2], items[3], items[4], items[5], SX, SY)
            source = items[7] - field if with_load else field
            solved = inexact_solve(source, items[6])
            return (solved[:, 0], solved[:, SX - 1], solved[:, :, 0], solved[:, :, SY - 1])
        outputs = lax.map(one_block, flat)
        return tuple((piece.reshape((n_depth, n_across) + piece.shape[1:]) for piece in outputs))

    def jumps(first_x, last_x, first_y, last_y):
        above = jnp.concatenate([first_x[1:], jnp.zeros_like(first_x[:1])], 0)
        return (last_x - above, last_y - jnp.roll(first_y, -1, axis=1), -first_x[:, :, 0] * mask_full)
    load_sums = jnp.sum(load_blocks, axis=(2, 3, 4)).T
    multipliers = lift(coarse_solve(normal_factor, tangent_factor, load_sums))
    gradient = tuple((-piece for piece in jumps(*traces(multipliers, True))))
    projected = project(gradient)
    norm_now = inner(projected, projected)
    direction = projected
    for step_index in range(ITERS):
        image = jumps(*traces(direction, False))
        step_size = norm_now / inner(direction, image)
        multipliers = combine(multipliers, direction, step_size)
        if step_index + 1 < ITERS:
            gradient = combine(gradient, image, step_size)
            projected = project(gradient)
            norm_next = inner(projected, projected)
            direction = combine(projected, direction, norm_next / norm_now)
            norm_now = norm_next
    lam_depth = multipliers[0].transpose(2, 0, 1, 3, 4).reshape(3, n_depth, n_across * SY, SZ)
    lam_surface = multipliers[1].transpose(2, 0, 3, 1, 4).reshape(3, n_depth * SX, n_across, SZ)
    lam_contact = multipliers[2].reshape(n_depth, n_across * SY, SZ)
    return (lam_depth, lam_surface, lam_contact)
```

```python
import functools

import jax
import jax.numpy as jnp
import numpy as np
from jax import lax
from jax.experimental import pallas as pl
from jax.experimental.pallas import tpu as pltpu
from jax.sharding import PartitionSpec as P

SWEEPS = 6
COUPLING_SCALE = (0.0, 1.0, 0.5, 0.25)
RELAXATION = 0.6
KEEP = 1.0 - RELAXATION
PLANE = [(dx, dy) for dx in (-1, 0, 1) for dy in (-1, 0, 1)]
SAME = [o for o in PLANE if o != (0, 0)]
HALF = [(0, 1), (1, -1), (1, 0), (1, 1)]
SUB, LANE = 8, 128
PLUS, MINUS = 8, 17
SLOTS = 9
FUNCS = 5
F32 = jnp.float32


def shift_up(t):
    lane = lax.broadcasted_iota(jnp.int32, t.shape, 1)
    r = pltpu.roll(t, 1, 1)
    return jnp.where(lane == 0, pltpu.roll(r, 1, 0), r)


def shift_down(t):
    lane = lax.broadcasted_iota(jnp.int32, t.shape, 1)
    r = pltpu.roll(t, LANE - 1, 1)
    return jnp.where(lane == LANE - 1, pltpu.roll(r, SUB - 1, 0), r)


def one(value):
    return jnp.sum(jnp.sum(value, axis=0, keepdims=True), axis=1, keepdims=True)


def tree(values):
    values = list(values)
    while len(values) > 1:
        values = [a + b for a, b in zip(values[::2], values[1::2])] + (
            values[-1:] if len(values) % 2 else [])
    return values[0]


def edge_weights(nx, ny, mod, mp, ms, e_ref):
    zero = jnp.zeros((SUB, LANE), F32)
    sub = lax.broadcasted_iota(jnp.int32, (SUB, LANE), 0)
    lane = lax.broadcasted_iota(jnp.int32, (SUB, LANE), 1)
    last = (sub == SUB - 1) & (lane == LANE - 1)
    for y in range(ny):
        for ref in (mp, ms):
            ref[0, y] = zero
            ref[nx + 1, y] = zero
        for n, (dx, dy) in enumerate(HALF):
            if dx == 1:
                e_ref[n, 0, y] = zero
        for n, (dx, dy) in enumerate(PLANE):
            if dx == 1:
                e_ref[4 + n, 0, y] = zero
            if dx == -1:
                e_ref[4 + n, nx + 1, y] = zero

    def fill(x, c):
        for y in range(ny):
            a = mod[x, y]
            mp[x + 1, y] = a
            ms[x + 1, y] = jnp.where(last, 0.0, shift_down(a))
        return c

    lax.fori_loop(0, nx, fill, 0)

    def row(x, c):
        for y in range(ny):
            a = mp[x + 1, y]
            scaled = {k: (2.0 * COUPLING_SCALE[k]) * a for k in (1, 2, 3)}
            for n, (dx, dy) in enumerate(HALF):
                if 0 <= y + dy < ny:
                    b = mp[x + 1 + dx, y + dy]
                    e_ref[n, x + 1, y] = scaled[abs(dx) + abs(dy)] * b / (a + b)
            for n, (dx, dy) in enumerate(PLANE):
                if 0 <= y + dy < ny:
                    b = ms[x + 1 + dx, y + dy]
                    e_ref[4 + n, x + 1, y] = scaled[abs(dx) + abs(dy) + 1] * b / (a + b)
        return c

    lax.fori_loop(0, nx, row, 0)


def scaled_weights(nx, ny, e_ref, w_ref, q_ref, p_ref):
    def row(x, c):
        for y in range(ny):
            w0, later, early = {}, {}, {}
            for d in SAME:
                dx, dy = d
                if 0 <= y + dy < ny:
                    if d in HALF:
                        w0[d] = e_ref[HALF.index(d), x + 1, y]
                    else:
                        w0[d] = e_ref[HALF.index((-dx, -dy)), x + 1 + dx, y + dy]
            for d in PLANE:
                dx, dy = d
                if 0 <= y + dy < ny:
                    later[d] = e_ref[4 + PLANE.index(d), x + 1, y]
                    early[d] = e_ref[4 + PLANE.index((-dx, -dy)), x + 1 + dx, y + dy]
            diag = tree(w0.values()) + tree(later.values()) + shift_up(tree(early.values()))
            q = RELAXATION / diag
            q_ref[x, y] = q
            p_ref[x, y] = diag * (1.0 / RELAXATION)
            qs = q * (1.0 / KEEP)
            qd = shift_down(qs)
            for d in w0:
                w_ref[x, y, SAME.index(d)] = qs * w0[d]
            for d in later:
                w_ref[x, y, PLUS + PLANE.index(d)] = shift_up(qs * later[d])
                w_ref[x, y, MINUS + PLANE.index(d)] = qd * early[d]
        return c

    lax.fori_loop(0, nx, row, 0)


def columns(x, ys, dxs, ny, src, w_ref, act):
    cache = {}

    def v(dx, y):
        if (dx, y) not in cache:
            cache[dx, y] = src[x + 1 + dx, y]
        return cache[dx, y]

    for y in ys:
        mid, plus, minus = None, None, None
        for dx in dxs:
            for dy in (-1, 0, 1):
                if not 0 <= y + dy < ny:
                    continue
                value = v(dx, y + dy)
                j = PLANE.index((dx, dy))
                wp, wm = w_ref[x, y, PLUS + j] * value, w_ref[x, y, MINUS + j] * value
                plus = wp if plus is None else plus + wp
                minus = wm if minus is None else minus + wm
                if (dx, dy) != (0, 0):
                    w = w_ref[x, y, SAME.index((dx, dy))] * value
                    mid = w if mid is None else mid + w
        act(x, y, v(0, y), mid + (shift_down(plus) + shift_up(minus)))
        for dx in dxs:
            cache.pop((dx, y - 1), None)


def region(nx, ny, depth, src, w_ref, act):
    inner = min(nx, 2 * (depth + 1)) - 2
    full = range(ny)
    columns(0, full, (0, 1), ny, src, w_ref, act)
    columns(nx - 1, full, (-1, 0), ny, src, w_ref, act)
    every = inner == nx - 2

    def row(i, c):
        x = i + 1 if every else jnp.where(i < depth, i + 1, i + 1 + (nx - 2 - inner))
        columns(x, full, (-1, 0, 1), ny, src, w_ref, act)
        return c

    if inner > 0:
        lax.fori_loop(0, inner, row, 0)
    if not every:
        for x in range(depth + 1, nx - 1 - depth):
            columns(x, range(0, depth + 1), (-1, 0, 1), ny, src, w_ref, act)
            columns(x, range(ny - 1 - depth, ny), (-1, 0, 1), ny, src, w_ref, act)


def face_columns(nx, ny):
    return ([(0, y) for y in range(ny)] + [(nx - 1, y) for y in range(ny)]
            + [(x, y) for x in range(1, nx - 1) for y in (0, ny - 1)])


def sweep(nx, ny, depth, src, dst, w_ref, source=None):
    def act(x, y, center, total):
        value = center + total
        if source is not None:
            value = value + source[0] * source[1][x, y]
        dst[x + 1, y] = value

    region(nx, ny, depth, src, w_ref, act)


def coarse_tables(nd, na, face_x, face_y):
    total = nd * na
    path = 2.0 * np.eye(nd) - np.eye(nd, k=1) - np.eye(nd, k=-1)
    path[0, 0] = 1.0
    eye = np.eye(na)
    cycle = 2.0 * eye - np.roll(eye, 1, axis=1) - np.roll(eye, -1, axis=1)
    inv = np.linalg.inv(face_x * np.kron(path, eye) + face_y * np.kron(np.eye(nd), cycle))
    ident = np.eye(total)
    up, right = np.kron(np.eye(nd, k=-1), eye), np.kron(np.eye(nd), np.roll(eye, 1, axis=0))
    part_x, part_y = ident - up, ident - right
    linked = ident.copy()
    linked[:na] = 0.0
    maps = [part_x, -part_x @ up.T, part_y, -part_y @ right.T, ident]
    out = np.zeros((nd, FUNCS + na + 2, nd, na, LANE))

    def at(b, s):
        return ident[(b * na + s % na)] if 0 <= b < nd else np.zeros(total)

    for b in range(nd):
        pick = [at(b, 0) - at(b + 1, 0), (at(b - 1, 0) - at(b, 0)) * (b > 0), at(b, 0) - at(b, 1),
                at(b, -1) - at(b, 0), at(b, 0)] + [at(0, f) for f in range(na)]
        for k, e in enumerate(pick):
            r = e @ inv
            for lane, m in enumerate(maps):
                out[b, k, :, :, lane] = (r @ m).reshape(nd, na)
            for lane in (8, 9, 10):
                out[b, k, :, :, lane] = r.reshape(nd, na)
            if k < FUNCS:
                out[b, FUNCS + na, 0, :, k] = r[:na]
        out[b, FUNCS + na + 1, 0, :, :na] = inv[:na, :na]
    return out


def feti_kernel(nx, ny, nz, nd, na, load_hbm, mod_hbm, act_hbm, maps_hbm, out_x, out_y, out_c,
                load, mod, act, maps, mask, mp, ms, e_ref, w_ref, q_ref, p_ref, ga, gb, la, lb,
                v0, f_ref, u_x, u_y, below_in, above_in, right_in, left_in,
                y_x, y_y, y_c, base_f, w_func, moments, sent, table, res_x, res_y, res_c,
                in_sem, out_sem, face_send, face_recv, row_send, near_recv, far_recv):
    body, surf = lax.axis_index("body"), lax.axis_index("surf")
    total = nd * na
    below, above = lax.rem(body + 1, nd), lax.rem(body + nd - 1, nd)
    right, left = lax.rem(surf + 1, na), lax.rem(surf + na - 1, na)
    mesh_id = pl.DeviceIdType.MESH
    inner = jnp.where(body > 0, 1.0, 0.0).astype(F32)
    outer = jnp.where(body < nd - 1, 1.0, 0.0).astype(F32)
    lane = lax.broadcasted_iota(jnp.int32, (SUB, LANE), 1)
    zero = jnp.zeros((SUB, LANE), F32)
    blocks = nz // LANE
    peer_surf = [lax.rem(surf + k, na) for k in range(na)]

    for zb in range(blocks):
        z = pl.ds(zb * LANE, LANE)
        pltpu.make_async_copy(mod_hbm.at[:, :, z], mod.at[:, :, zb, :], in_sem.at[3]).start()
    for zb in range(blocks):
        z = pl.ds(zb * LANE, LANE)
        for c in range(3):
            pltpu.make_async_copy(load_hbm.at[c, :, :, z], load.at[c, :, :, zb, :], in_sem.at[c]).start()
        pltpu.make_async_copy(act_hbm.at[:, z], act.at[:, zb, :], in_sem.at[4]).start()
    maps_copy = pltpu.make_async_copy(maps_hbm.at[body], maps, in_sem.at[5])
    maps_copy.start()

    def every_peer(do):
        for k in range(1, na):
            do(k, body, peer_surf[k], True)

        def others(d, c):
            there = lax.rem(body + d, nd)
            for k in range(na):
                do(k, there, peer_surf[k], False)
            return c

        lax.fori_loop(1, nd, others, 0)

    barrier = pltpu.get_barrier_semaphore()
    every_peer(lambda k, b, s, near: pl.semaphore_signal(
        barrier, inc=1, device_id=(b, s), device_id_type=mesh_id))

    def post(slot, values):
        row = jnp.zeros((SUB, LANE), F32)
        for k, value in values:
            row = jnp.where(lane == k, value, row)
        sent[slot] = row
        table[slot, body, pl.ds(0, 1)] = row[0:1]

        def send(k, b, s, near):
            pltpu.make_async_remote_copy(
                src_ref=sent.at[slot, pl.ds(0, 1)], dst_ref=table.at[slot, body, pl.ds((na - k) % na, 1)],
                send_sem=row_send.at[slot], recv_sem=(near_recv if near else far_recv).at[slot],
                device_id=(b, s), device_id_type=mesh_id).start()

        every_peer(send)

    def row_wait(slot, ref, sem):
        return pltpu.make_async_remote_copy(
            src_ref=ref, dst_ref=ref, send_sem=row_send.at[slot], recv_sem=sem.at[slot],
            device_id=(body, right), device_id_type=mesh_id)

    def collect(slot):
        row_wait(slot, table.at[slot, 0, pl.ds(0, na - 1)], near_recv).wait_recv()
        row_wait(slot, table.at[slot, pl.ds(0, nd - 1)], far_recv).wait_recv()

    def sent_all(slot):
        row_wait(slot, table.at[slot, 0, pl.ds(0, na - 1)], near_recv).wait_send()
        row_wait(slot, table.at[slot, pl.ds(0, nd - 1)], far_recv).wait_send()

    def faces(slot):
        def copy(i, src, dst, peer):
            return pltpu.make_async_remote_copy(
                src_ref=src, dst_ref=dst, send_sem=face_send.at[slot, i], recv_sem=face_recv.at[slot, i],
                device_id=peer, device_id_type=mesh_id)

        return (copy(0, u_y.at[slot, 1], right_in.at[slot], (body, left)),
                copy(1, u_y.at[slot, 0], left_in.at[slot], (body, right)),
                copy(2, u_x.at[slot, 1], below_in.at[slot], (above, surf)),
                copy(3, u_x.at[slot, 0], above_in.at[slot], (below, surf)))

    def start_faces(slot):
        to_left, to_right, to_above, to_below = faces(slot)
        to_left.start()
        to_right.start()
        pl.when(body > 0)(to_above.start)
        pl.when(body < nd - 1)(to_below.start)

    def wait_faces(slot):
        to_left, to_right, to_above, to_below = faces(slot)
        to_left.wait_recv()
        to_right.wait_recv()
        pl.when(body < nd - 1)(to_above.wait_recv)
        pl.when(body > 0)(to_below.wait_recv)

    def faces_sent(slot):
        to_left, to_right, to_above, to_below = faces(slot)
        to_left.wait_send()
        to_right.wait_send()
        pl.when(body > 0)(to_above.wait_send)
        pl.when(body < nd - 1)(to_below.wait_send)

    @pl.when(body == 0)
    def _():
        above_in[...] = jnp.zeros_like(above_in)

    @pl.when(body == nd - 1)
    def _():
        below_in[...] = jnp.zeros_like(below_in)

    def arrived(ref, sem):
        pltpu.make_async_copy(ref, ref, in_sem.at[sem]).wait()

    arrived(mod, 3)
    edge_weights(nx, ny, mod, mp, ms, e_ref)
    for c in range(3):
        arrived(load.at[c], c)
    arrived(act, 4)
    top = jnp.where(body == 0, 1.0, 0.0).astype(F32)
    count = zero
    for y in range(ny):
        mask[y] = act[y].astype(F32) * top
        count = count + mask[y]

    def load_row(x, sums):
        return tuple(s + tree([load[c, x, y] for y in range(ny)]) for c, s in enumerate(sums))

    load_sums = lax.fori_loop(0, nx, load_row, (zero,) * 3)
    pl.semaphore_wait(barrier, total - 1)
    post(SLOTS, [(8 + c, one(load_sums[c])) for c in range(3)] + [(11, one(count))])
    scaled_weights(nx, ny, e_ref, w_ref, q_ref, p_ref)

    def clear(x, c):
        for ref in (ga, gb, la, lb):
            for y in range(ny):
                ref[x, y] = zero
        return c

    lax.fori_loop(0, nx + 2, clear, 0)
    moments[...] = jnp.zeros_like(moments)
    maps_copy.wait()
    collect(SLOTS)

    rows = table[SLOTS]
    counts = jnp.sum(jnp.where(lax.broadcasted_iota(jnp.int32, (na, LANE), 1) == 11, rows[0], 0.0),
                     axis=1, keepdims=True)
    sq_row = lax.broadcasted_iota(jnp.int32, (na, LANE), 0)
    sq_col = lax.broadcasted_iota(jnp.int32, (na, LANE), 1)
    work = jnp.where(sq_row == sq_col, 1.0, 0.0) + counts * maps[FUNCS + na + 1, 0]
    other = counts * maps[FUNCS + na, 0]
    row_id = lax.broadcasted_iota(jnp.int32, (na, 1), 0)
    for k in range(na):
        scale = 1.0 / work[k : k + 1, k : k + 1]
        pivot, tail = work[k : k + 1] * scale, other[k : k + 1] * scale
        factor = work[:, k : k + 1]
        work = jnp.where(row_id == k, pivot, work - factor * pivot)
        other = jnp.where(row_id == k, tail, other - factor * tail)
    for k in range(FUNCS):
        plain = maps[k]
        w_func[1, k] = plain
        w_func[0, k] = plain - tree([other[f : f + 1, k : k + 1] * maps[FUNCS + f] for f in range(na)])

    wide = lax.broadcasted_iota(jnp.int32, (nd, na, LANE), 2)
    for c in range(3):
        own = jnp.where(wide == 8 + c, rows, 0.0)
        for k in range(FUNCS):
            base_f[c, k] = jnp.broadcast_to(one(jnp.sum(w_func[min(c, 1), k] * own, axis=0)), (SUB, LANE))

    scales = [KEEP ** k for k in range(SWEEPS)]
    depths = [min((min(nx, ny) - 1) // 2, SWEEPS - 1 - k) for k in range(SWEEPS)]

    def finish(slot, h, values):
        last = scales[SWEEPS - 1]

        def u(x, y):
            return last * h[x + 1, y] + v0[x, y]

        sums = [[], [], [], []]
        for x in range(nx):
            for side, y in ((0, ny - 1), (1, 0)):
                value = u(x, y)
                u_y[slot, side, x] = value
                sums[2 + side].append(value)
        contact = []
        for y in range(ny):
            for side, x in ((0, nx - 1), (1, 0)):
                value = u(x, y)
                u_x[slot, side, y] = value
                sums[side].append(value)
                if side:
                    contact.append(mask[y] * value)
        start_faces(slot)
        normal = jnp.where(lax.rem(slot, 3) == 0, 1.0, 0.0).astype(F32)
        post(slot, [(k, one(tree(s))) for k, s in enumerate(sums)] + [(4, normal * one(tree(contact)))])

    def first(c, carry):
        fs = [base_f[c, k] for k in range(FUNCS)]
        normal = jnp.where(c == 0, 1.0, 0.0).astype(F32)

        def fill(x, carry):
            for y in range(ny):
                value = q_ref[x, y] * load[c, x, y]
                v0[x, y] = value
                ga[x + 1, y] = value
            return carry

        lax.fori_loop(0, nx, fill, 0)
        for x, y in face_columns(nx, ny):
            f = zero
            if x == nx - 1:
                f = f + fs[0]
            if x == 0:
                f = f - fs[1] + (normal * fs[4]) * mask[y]
            if y == ny - 1:
                f = f + fs[2]
            if y == 0:
                f = f - fs[3]
            value = v0[x, y] - q_ref[x, y] * f
            v0[x, y] = value
            ga[x + 1, y] = value
        bufs = (ga, gb)
        for k in range(1, SWEEPS):
            source = None if k == SWEEPS - 1 else (1.0 / scales[k], v0)
            sweep(nx, ny, depths[k], bufs[(k - 1) % 2], bufs[k % 2], w_ref, source)
        finish(c, bufs[(SWEEPS - 1) % 2], None)
        return carry

    lax.fori_loop(0, 3, first, 0)

    def project(slot):
        wait_faces(slot)
        collect(slot)
        c = lax.rem(slot, 3)
        power = lax.div(slot, 3)
        kind = jnp.minimum(c, 1)
        sign = jnp.where(slot < 3, -1.0, 1.0).astype(F32)
        normal = jnp.where(c == 0, 1.0, 0.0).astype(F32)
        tab = table[slot]
        fs = [sign * one(jnp.sum(w_func[kind, k] * tab, axis=0)) for k in range(FUNCS)]
        fs = [jnp.broadcast_to(f, (SUB, LANE)) for f in fs]
        field, squares = {}, []

        def put(x, y, value):
            field[x, y] = value if (x, y) not in field else field[x, y] + value

        for y in range(ny):
            head = u_x[slot, 1, y]
            own = sign * (u_x[slot, 0, y] - outer * below_in[slot, y]) - fs[0]
            up = (sign * inner) * (above_in[slot, y] - head) - fs[1]
            touch = normal * mask[y] * (fs[4] - sign * head)
            y_x[slot, 0, y] = own
            y_x[slot, 1, y] = up
            y_c[slot, y] = touch
            squares += [own * own, touch * touch]
            put(nx - 1, y, own)
            put(0, y, -up - touch)
        for x in range(nx):
            own = sign * (u_y[slot, 0, x] - right_in[slot, x]) - fs[2]
            up = sign * (left_in[slot, x] - u_y[slot, 1, x]) - fs[3]
            y_y[slot, 0, x] = own
            y_y[slot, 1, x] = up
            squares.append(own * own)
            put(x, ny - 1, own)
            put(x, 0, -up)
        moments[2 * power] = moments[2 * power] + tree(squares)
        for (x, y), value in field.items():
            f_ref[x, y] = value
            value = q_ref[x, y] * value
            v0[x, y] = value
            la[x + 1, y] = value

    edge = face_columns(nx, ny)
    deep = {d: [(x, y) for x in range(nx) for y in range(ny) if min(x, nx - 1 - x, y, ny - 1 - y) == d]
            for d in (1, 2)}

    def add_source(k, dst):
        for x, y in edge:
            dst[x + 1, y] = dst[x + 1, y] + (1.0 / scales[k]) * v0[x, y]

    def clean():
        for x, y in deep[1]:
            la[x + 1, y] = zero
        for x, y in deep[2]:
            la[x + 1, y] = zero
            lb[x + 1, y] = zero

    def krylov(i, carry):
        clean()
        project(i)
        bufs = (la, lb)
        for k in range(1, SWEEPS):
            sweep(nx, ny, min(k, depths[k]), bufs[(k - 1) % 2], bufs[k % 2], w_ref)
            if k < SWEEPS - 1:
                add_source(k, bufs[k % 2])
        slot = i + 3
        finish(slot, bufs[(SWEEPS - 1) % 2], None)
        parts = []
        for y in range(ny):
            parts += [y_x[i, 0, y] * u_x[slot, 0, y], -(y_x[i, 1, y] + y_c[i, y]) * u_x[slot, 1, y]]
        for x in range(nx):
            parts += [y_y[i, 0, x] * u_y[slot, 0, x], -y_y[i, 1, x] * u_y[slot, 1, x]]
        odd = 2 * lax.div(i, 3) + 1
        moments[odd] = moments[odd] + tree(parts)
        return carry

    lax.fori_loop(0, 6, krylov, 0)

    def last_moment(i, carry):
        clean()
        project(i)
        sweep(nx, ny, 1, la, lb, w_ref)
        add_source(1, lb)
        sweep(nx, ny, 2, lb, la, w_ref)
        add_source(2, la)
        square = scales[2] * scales[2]

        def act_on(x, y, center, around):
            moments[6] = moments[6] + (p_ref[x, y] * center) * (
                (-RELAXATION * square) * center + (KEEP * square) * around)

        moments[6] = zero
        region(nx, ny, 2, la, w_ref, act_on)
        parts = [f_ref[x, y] * la[x + 1, y] for x, y in edge]
        moments[5] = moments[5] + moments[6] + (2.0 * scales[2]) * tree(parts)
        return carry

    lax.fori_loop(6, 9, last_moment, 0)
    post(SLOTS + 1, [(j, one(moments[j])) for j in range(6)])
    collect(SLOTS + 1)
    sums = jnp.sum(jnp.sum(table[SLOTS + 1], axis=0), axis=0, keepdims=True)
    m = [jnp.broadcast_to(sums[:, j : j + 1], (1, LANE)) for j in range(6)]

    a0 = m[0] / m[1]
    g1 = m[0] + 2.0 * a0 * m[1] + a0 * a0 * m[2]
    c1 = 1.0 + g1 / m[0]
    a1 = g1 / (c1 * c1 * m[1] + 2.0 * c1 * a0 * m[2] + a0 * a0 * m[3])
    pp, ss = a0 + a1 * c1, a1 * a0
    g2 = m[0] + 2.0 * pp * m[1] + (pp * pp + 2.0 * ss) * m[2] + 2.0 * pp * ss * m[3] + ss * ss * m[4]
    b2 = g2 / g1
    da, db = 1.0 + b2 * c1, pp + b2 * a0
    a2 = g2 / (da * da * m[1] + 2.0 * da * db * m[2] + (db * db + 2.0 * da * ss) * m[3]
               + 2.0 * db * ss * m[4] + ss * ss * m[5])
    k0 = jnp.broadcast_to(a0 + a1 * c1 + a2 * da, (SUB, LANE))
    k1 = jnp.broadcast_to(a1 * a0 + a2 * db, (SUB, LANE))
    k2 = jnp.broadcast_to(a2 * ss, (SUB, LANE))

    for c in range(3):
        for y in range(ny):
            res_x[c, y] = base_f[c, 0] + (k0 * y_x[c, 0, y] + k1 * y_x[3 + c, 0, y] + k2 * y_x[6 + c, 0, y])
        for x in range(nx):
            res_y[c, x] = base_f[c, 2] + (k0 * y_y[c, 0, x] + k1 * y_y[3 + c, 0, x] + k2 * y_y[6 + c, 0, x])
    for y in range(ny):
        res_c[y] = (k0 * y_c[0, y] + k1 * y_c[3, y] + k2 * y_c[6, y]) - base_f[0, 4] * mask[y]
    for zb in range(blocks):
        z = pl.ds(zb * LANE, LANE)
        pltpu.make_async_copy(res_x.at[:, :, zb, :], out_x.at[:, 0, :, z], out_sem.at[0]).start()
        pltpu.make_async_copy(res_y.at[:, :, zb, :], out_y.at[:, :, 0, z], out_sem.at[1]).start()
        pltpu.make_async_copy(res_c.at[:, zb, :], out_c.at[0, :, z], out_sem.at[2]).start()
    for k, ref in enumerate((res_x, res_y, res_c)):
        pltpu.make_async_copy(ref, ref, out_sem.at[k]).wait()

    def drain(slot, c):
        faces_sent(slot)
        sent_all(slot)
        return c

    lax.fori_loop(0, SLOTS, drain, 0)
    sent_all(SLOTS)
    sent_all(SLOTS + 1)


def shards(external_load, modulus, active):
    nx, ny, nz = modulus.shape
    nd, na = lax.axis_size("body"), lax.axis_size("surf")
    maps = jnp.asarray(coarse_tables(nd, na, float(ny * nz), float(nx * nz)), F32)
    tile = (SUB, LANE)
    padded, grid = (nx + 2, ny) + tile, (nx, ny) + tile
    any_spec = pl.BlockSpec(memory_space=pl.ANY)
    shapes = [
        ((3,) + grid, F32), (grid, F32), ((ny,) + tile, jnp.int32), ((FUNCS + na + 2, nd, na, LANE), F32),
        ((ny,) + tile, F32), (padded, F32), (padded, F32), ((13,) + padded, F32), (grid[:2] + (26,) + tile, F32),
        (grid, F32), (grid, F32), (padded, F32), (padded, F32), (padded, F32), (padded, F32),
        (grid, F32), (grid, F32), ((SLOTS, 2, ny) + tile, F32), ((SLOTS, 2, nx) + tile, F32),
        ((SLOTS, ny) + tile, F32), ((SLOTS, ny) + tile, F32), ((SLOTS, nx) + tile, F32), ((SLOTS, nx) + tile, F32),
        ((SLOTS, 2, ny) + tile, F32), ((SLOTS, 2, nx) + tile, F32), ((SLOTS, ny) + tile, F32),
        ((3, FUNCS) + tile, F32), ((2, FUNCS, nd, na, LANE), F32), ((7,) + tile, F32),
        ((SLOTS + 2,) + tile, F32), ((SLOTS + 2, nd, na, LANE), F32),
        ((3, ny) + tile, F32), ((3, nx) + tile, F32), ((ny,) + tile, F32)]
    dma = pltpu.SemaphoreType.DMA
    return pl.pallas_call(
        functools.partial(feti_kernel, nx, ny, nz, nd, na),
        out_shape=(jax.ShapeDtypeStruct((3, 1, ny, nz), F32), jax.ShapeDtypeStruct((3, nx, 1, nz), F32),
                   jax.ShapeDtypeStruct((1, ny, nz), F32)),
        in_specs=[any_spec] * 4, out_specs=(any_spec,) * 3,
        scratch_shapes=[pltpu.VMEM(s, t) for s, t in shapes] + [
            dma((6,)), dma((3,)), dma((SLOTS, 4)), dma((SLOTS, 4)),
            dma((SLOTS + 2,)), dma((SLOTS + 2,)), dma((SLOTS + 2,))],
        compiler_params=pltpu.CompilerParams(
            vmem_limit_bytes=56 * 1024 * 1024, collective_id=0, has_side_effects=True),
    )(external_load, modulus, active, maps)


def solution(mesh):
    placed = (P(None, "body", "surf", None), P("body", "surf", None), P("surf", None))
    return jax.shard_map(
        shards,
        mesh=mesh,
        in_specs=placed,
        out_specs=(
            P(None, "body", "surf", None),
            P(None, "body", "surf", None),
            P("body", "surf", None),
        ),
        check_vma=False,
    )
```

```python
import functools

import jax
import jax.numpy as jnp
import numpy as np
from jax import lax
from jax.experimental import pallas as pl
from jax.experimental.pallas import tpu as pltpu
from jax.sharding import PartitionSpec as P

SWEEPS = 6
COUPLING_SCALE = (0.0, 1.0, 0.5, 0.25)
RELAXATION = 0.6
KEEP = 1.0 - RELAXATION
PLANE = [(dx, dy) for dx in (-1, 0, 1) for dy in (-1, 0, 1)]
SAME = [o for o in PLANE if o != (0, 0)]
HALF = [(0, 1), (1, -1), (1, 0), (1, 1)]
SUB, LANE = 8, 128
PLUS, MINUS = 8, 17
SLOTS = 9
WIDE = 7
FUNCS = 5
F32 = jnp.float32


def shift(t, by, edge):
    axis = t.ndim - 1
    lane = lax.broadcasted_iota(jnp.int32, t.shape, axis)
    r = pltpu.roll(t, by % LANE, axis)
    return jnp.where(lane == edge, pltpu.roll(r, by % SUB, axis - 1), r)


def shift_up(t):
    return shift(t, 1, 0)


def shift_down(t):
    return shift(t, -1, LANE - 1)


def one(value):
    return jnp.sum(jnp.sum(value, axis=0, keepdims=True), axis=1, keepdims=True)


def rows_by_two(nx, act):
    def pair(i, c):
        act(2 * i)
        act(2 * i + 1)
        return c

    lax.fori_loop(0, nx // 2, pair, 0)
    if nx % 2:
        act(nx - 1)


def tree(values):
    values = list(values)
    while len(values) > 1:
        values = [a + b for a, b in zip(values[::2], values[1::2])] + (
            values[-1:] if len(values) % 2 else [])
    return values[0]


def edge_weights(nx, ny, mod, mp, ms, e_ref):
    zero = jnp.zeros((SUB, LANE), F32)
    sub = lax.broadcasted_iota(jnp.int32, (SUB, LANE), 0)
    lane = lax.broadcasted_iota(jnp.int32, (SUB, LANE), 1)
    last = (sub == SUB - 1) & (lane == LANE - 1)
    for y in range(ny):
        for ref in (mp, ms):
            ref[0, y] = zero
            ref[nx + 1, y] = zero
        for n, (dx, dy) in enumerate(HALF):
            if dx == 1:
                e_ref[n, 0, y] = zero
        for n, (dx, dy) in enumerate(PLANE):
            if dx == 1:
                e_ref[4 + n, 0, y] = zero
            if dx == -1:
                e_ref[4 + n, nx + 1, y] = zero

    def fill(x):
        for y in range(ny):
            a = mod[x, y]
            mp[x + 1, y] = a
            ms[x + 1, y] = jnp.where(last, 0.0, shift_down(a))

    rows_by_two(nx, fill)

    def row(x):
        for first, dirs, other in ((0, HALF, mp), (4, PLANE, ms)):
            for n, (dx, dy) in enumerate(dirs):
                lo, hi = max(0, -dy), ny - max(0, dy)
                a, b = mp[x + 1, pl.ds(lo, hi - lo)], other[x + 1 + dx, pl.ds(lo + dy, hi - lo)]
                scale = 2.0 * COUPLING_SCALE[abs(dx) + abs(dy) + (first > 0)]
                e_ref[first + n, x + 1, pl.ds(lo, hi - lo)] = (scale * a) * b / (a + b)

    rows_by_two(nx, row)


def same_edges(d, x, lo, count, e_ref):
    if d in HALF:
        return e_ref[HALF.index(d), x + 1, pl.ds(lo, count)]
    return e_ref[HALF.index((-d[0], -d[1])), x + 1 + d[0], pl.ds(lo + d[1], count)]


def early_edges(d, x, lo, count, e_ref):
    return e_ref[4 + PLANE.index((-d[0], -d[1])), x + 1 + d[0], pl.ds(lo + d[1], count)]


def scaled_weights(nx, ny, mp, e_ref, w_ref, q_ref, p_ref):
    sub = lax.broadcasted_iota(jnp.int32, (ny, SUB, LANE), 1)
    lane = lax.broadcasted_iota(jnp.int32, (ny, SUB, LANE), 2)
    start = (sub == 0) & (lane == 0)

    def diagonal(x):
        for lo, count in runs(range(ny), lambda y: (y == 0, y == ny - 1)):
            valid = [d for d in PLANE if 0 <= lo + d[1] and lo + count + d[1] <= ny]
            later = tree([same_edges(d, x, lo, count, e_ref) for d in valid if d != (0, 0)]
                         + [e_ref[4 + PLANE.index(d), x + 1, pl.ds(lo, count)] for d in valid])
            diag = later + shift_up(tree([early_edges(d, x, lo, count, e_ref) for d in valid]))
            q_ref[x, pl.ds(lo, count)] = RELAXATION / diag
            p_ref[x, pl.ds(lo, count)] = diag * (1.0 / RELAXATION)

    def scale(x):
        qs = q_ref[x] * (1.0 / KEEP)
        qd = shift_down(qs)
        a = jnp.where(start, 0.0, shift_up(mp[x + 1, pl.ds(0, ny)]))
        qa = shift_up(qs) * a
        for j, d in enumerate(PLANE):
            lo, hi = max(0, -d[1]), ny - max(0, d[1])
            ys = pl.ds(lo, hi - lo)
            if d != (0, 0):
                w_ref[x, ys, SAME.index(d)] = qs[lo:hi] * same_edges(d, x, lo, hi - lo, e_ref)
            b = mp[x + 1 + d[0], pl.ds(lo + d[1], hi - lo)]
            c = 2.0 * COUPLING_SCALE[abs(d[0]) + abs(d[1]) + 1]
            w_ref[x, ys, PLUS + j] = (c * qa[lo:hi]) * b / (a[lo:hi] + b)
            w_ref[x, ys, MINUS + j] = qd[lo:hi] * early_edges(d, x, lo, hi - lo, e_ref)

    rows_by_two(nx, diagonal)
    rows_by_two(nx, scale)


def to_face(x, y, nx, ny):
    return min(x, nx - 1 - x, y, ny - 1 - y)


def runs(ys, kind):
    out = []
    for y in ys:
        if out and out[-1][2] == kind(y) and out[-1][1] < WIDE:
            out[-1][1] += 1
        else:
            out.append([y, 1, kind(y)])
    return [(lo, count) for lo, count, _ in out]


def columns(x, ys, nx, ny, support, src, w_ref, act):
    def terms(y):
        return [d for d in PLANE if 0 <= to_face(x + d[0], y + d[1], nx, ny) <= support]

    for lo, count in runs(ys, lambda y: (terms(y), to_face(x, y, nx, ny) == 0)):
        at = pl.ds(lo, count)
        mid, plus, minus, center = None, None, None, None
        for dx, dy in terms(lo):
            j = PLANE.index((dx, dy))
            value = src[x + 1 + dx, pl.ds(lo + dy, count)]
            wp, wm = w_ref[x, at, PLUS + j] * value, w_ref[x, at, MINUS + j] * value
            plus = wp if plus is None else plus + wp
            minus = wm if minus is None else minus + wm
            if (dx, dy) == (0, 0):
                center = value
            else:
                w = w_ref[x, at, SAME.index((dx, dy))] * value
                mid = w if mid is None else mid + w
        act(x, lo, count, center, mid + (shift_down(plus) + shift_up(minus)))


def region(nx, ny, depth, support, src, w_ref, act):
    for x in range(nx):
        near = min(x, nx - 1 - x) <= depth
        for ys in [range(ny)] if near else [range(0, depth + 1), range(ny - 1 - depth, ny)]:
            columns(x, ys, nx, ny, support, src, w_ref, act)


def face_columns(nx, ny):
    return ([(0, y) for y in range(ny)] + [(nx - 1, y) for y in range(ny)]
            + [(x, y) for x in range(1, nx - 1) for y in (0, ny - 1)])


def sweep(nx, ny, depth, support, src, dst, w_ref, scale, v0, reach, last=False):
    def act(x, lo, count, center, total):
        value = total if center is None else center + total
        if not last and to_face(x, lo, nx, ny) <= reach:
            value = value + scale * v0[x, pl.ds(lo, count)]
        dst[x + 1, pl.ds(lo, count)] = value

    region(nx, ny, depth, support, src, w_ref, act)


def coarse_tables(nd, na, face_x, face_y):
    total = nd * na
    path = 2.0 * np.eye(nd) - np.eye(nd, k=1) - np.eye(nd, k=-1)
    path[0, 0] = 1.0
    eye = np.eye(na)
    cycle = 2.0 * eye - np.roll(eye, 1, axis=1) - np.roll(eye, -1, axis=1)
    inv = np.linalg.inv(face_x * np.kron(path, eye) + face_y * np.kron(np.eye(nd), cycle))
    ident = np.eye(total)
    up, right = np.kron(np.eye(nd, k=-1), eye), np.kron(np.eye(nd), np.roll(eye, 1, axis=0))
    part_x, part_y = ident - up, ident - right
    linked = ident.copy()
    linked[:na] = 0.0
    maps = [part_x, -part_x @ up.T, part_y, -part_y @ right.T, ident]
    out = np.zeros((nd, FUNCS + na + 2, nd, na, LANE))

    def at(b, s):
        return ident[(b * na + s % na)] if 0 <= b < nd else np.zeros(total)

    for b in range(nd):
        pick = [at(b, 0) - at(b + 1, 0), (at(b - 1, 0) - at(b, 0)) * (b > 0), at(b, 0) - at(b, 1),
                at(b, -1) - at(b, 0), at(b, 0)] + [at(0, f) for f in range(na)]
        for k, e in enumerate(pick):
            r = e @ inv
            for lane, m in enumerate(maps):
                out[b, k, :, :, lane] = (r @ m).reshape(nd, na)
            for lane in (8, 9, 10):
                out[b, k, :, :, lane] = r.reshape(nd, na)
            if k < FUNCS:
                out[b, FUNCS + na, 0, :, k] = r[:na]
        out[b, FUNCS + na + 1, 0, :, :na] = inv[:na, :na]
    return out


def feti_kernel(nx, ny, nz, nd, na, load_hbm, mod_hbm, act_hbm, maps_hbm, out_x, out_y, out_c,
                load, mod, act, maps, mask, mp, ms, e_ref, w_ref, q_ref, p_ref, ga, gb, la, lb,
                v0, f_ref, u_x, u_y, below_in, above_in, right_in, left_in,
                y_x, y_y, y_c, base_f, w_func, moments, sent, table, res_x, res_y, res_c,
                in_sem, out_sem, face_send, face_recv, row_send, near_recv, far_recv):
    body, surf = lax.axis_index("body"), lax.axis_index("surf")
    total = nd * na
    below, above = lax.rem(body + 1, nd), lax.rem(body + nd - 1, nd)
    right, left = lax.rem(surf + 1, na), lax.rem(surf + na - 1, na)
    mesh_id = pl.DeviceIdType.MESH
    inner = jnp.where(body > 0, 1.0, 0.0).astype(F32)
    outer = jnp.where(body < nd - 1, 1.0, 0.0).astype(F32)
    lane = lax.broadcasted_iota(jnp.int32, (SUB, LANE), 1)
    zero = jnp.zeros((SUB, LANE), F32)
    blocks = nz // LANE
    peer_surf = [lax.rem(surf + k, na) for k in range(na)]

    def every_peer(do):
        for k in range(1, na):
            do(k, body, peer_surf[k], True)

        def others(d, c):
            there = lax.rem(body + d, nd)
            for k in range(na):
                do(k, there, peer_surf[k], False)
            return c

        lax.fori_loop(1, nd, others, 0)

    barrier = pltpu.get_barrier_semaphore()
    every_peer(lambda k, b, s, near: pl.semaphore_signal(
        barrier, inc=1, device_id=(b, s), device_id_type=mesh_id))

    for zb in range(blocks):
        z = pl.ds(zb * LANE, LANE)
        for c in range(3):
            pltpu.make_async_copy(load_hbm.at[c, :, :, z], load.at[c, :, :, zb, :], in_sem.at[3 + c]).start()
        pltpu.make_async_copy(act_hbm.at[:, z], act.at[:, zb, :], in_sem.at[0]).start()
    for zb in range(blocks):
        z = pl.ds(zb * LANE, LANE)
        pltpu.make_async_copy(mod_hbm.at[:, :, z], mod.at[:, :, zb, :], in_sem.at[1]).start()
    maps_copy = pltpu.make_async_copy(maps_hbm.at[body], maps, in_sem.at[2])
    maps_copy.start()

    def post(slot, values):
        row = jnp.zeros((SUB, LANE), F32)
        for k, value in values:
            row = jnp.where(lane == k, value, row)
        sent[slot] = row
        table[slot, body, pl.ds(0, 1)] = row[0:1]

        def send(k, b, s, near):
            pltpu.make_async_remote_copy(
                src_ref=sent.at[slot, pl.ds(0, 1)], dst_ref=table.at[slot, body, pl.ds((na - k) % na, 1)],
                send_sem=row_send.at[slot], recv_sem=(near_recv if near else far_recv).at[slot],
                device_id=(b, s), device_id_type=mesh_id).start()

        every_peer(send)

    def row_wait(slot, ref, sem):
        return pltpu.make_async_remote_copy(
            src_ref=ref, dst_ref=ref, send_sem=row_send.at[slot], recv_sem=sem.at[slot],
            device_id=(body, right), device_id_type=mesh_id)

    def collect(slot):
        row_wait(slot, table.at[slot, 0, pl.ds(0, na - 1)], near_recv).wait_recv()
        row_wait(slot, table.at[slot, pl.ds(0, nd - 1)], far_recv).wait_recv()

    def sent_all(slot):
        row_wait(slot, table.at[slot, 0, pl.ds(0, na - 1)], near_recv).wait_send()
        row_wait(slot, table.at[slot, pl.ds(0, nd - 1)], far_recv).wait_send()

    def faces(slot):
        def copy(i, src, dst, peer):
            return pltpu.make_async_remote_copy(
                src_ref=src, dst_ref=dst, send_sem=face_send.at[slot, i], recv_sem=face_recv.at[slot, i],
                device_id=peer, device_id_type=mesh_id)

        return (copy(0, u_y.at[slot, 1], right_in.at[slot], (body, left)),
                copy(1, u_y.at[slot, 0], left_in.at[slot], (body, right)),
                copy(2, u_x.at[slot, 1], below_in.at[slot], (above, surf)),
                copy(3, u_x.at[slot, 0], above_in.at[slot], (below, surf)))

    def start_faces(slot):
        to_left, to_right, to_above, to_below = faces(slot)
        to_left.start()
        to_right.start()
        pl.when(body > 0)(to_above.start)
        pl.when(body < nd - 1)(to_below.start)

    def wait_faces(slot):
        to_left, to_right, to_above, to_below = faces(slot)
        to_left.wait_recv()
        to_right.wait_recv()
        pl.when(body < nd - 1)(to_above.wait_recv)
        pl.when(body > 0)(to_below.wait_recv)

    def faces_sent(slot):
        to_left, to_right, to_above, to_below = faces(slot)
        to_left.wait_send()
        to_right.wait_send()
        pl.when(body > 0)(to_above.wait_send)
        pl.when(body < nd - 1)(to_below.wait_send)

    @pl.when(body == 0)
    def _():
        above_in[...] = jnp.zeros_like(above_in)

    @pl.when(body == nd - 1)
    def _():
        below_in[...] = jnp.zeros_like(below_in)

    def arrived(ref, sem):
        pltpu.make_async_copy(ref, ref, in_sem.at[sem]).wait()

    for c in range(3):
        arrived(load.at[c], 3 + c)
    arrived(act, 0)
    top = jnp.where(body == 0, 1.0, 0.0).astype(F32)
    count = zero
    for y in range(ny):
        mask[y] = act[y].astype(F32) * top
        count = count + mask[y]

    def load_row(x, sums):
        return tuple(s + tree([load[c, x, y] for y in range(ny)]) for c, s in enumerate(sums))

    load_sums = lax.fori_loop(0, nx, load_row, (zero,) * 3)
    pl.semaphore_wait(barrier, total - 1)
    post(SLOTS, [(8 + c, one(load_sums[c])) for c in range(3)] + [(11, one(count))])
    arrived(mod, 1)
    edge_weights(nx, ny, mod, mp, ms, e_ref)
    scaled_weights(nx, ny, mp, e_ref, w_ref, q_ref, p_ref)

    moments[...] = jnp.zeros_like(moments)
    maps_copy.wait()
    collect(SLOTS)

    rows = table[SLOTS]
    counts = jnp.sum(jnp.where(lax.broadcasted_iota(jnp.int32, (na, LANE), 1) == 11, rows[0], 0.0),
                     axis=1, keepdims=True)
    sq_row = lax.broadcasted_iota(jnp.int32, (na, LANE), 0)
    sq_col = lax.broadcasted_iota(jnp.int32, (na, LANE), 1)
    work = jnp.where(sq_row == sq_col, 1.0, 0.0) + counts * maps[FUNCS + na + 1, 0]
    other = counts * maps[FUNCS + na, 0]
    row_id = lax.broadcasted_iota(jnp.int32, (na, 1), 0)
    for k in range(na):
        scale = 1.0 / work[k : k + 1, k : k + 1]
        pivot, tail = work[k : k + 1] * scale, other[k : k + 1] * scale
        factor = work[:, k : k + 1]
        work = jnp.where(row_id == k, pivot, work - factor * pivot)
        other = jnp.where(row_id == k, tail, other - factor * tail)
    for k in range(FUNCS):
        plain = maps[k]
        w_func[1, k] = plain
        w_func[0, k] = plain - tree([other[f : f + 1, k : k + 1] * maps[FUNCS + f] for f in range(na)])

    wide = lax.broadcasted_iota(jnp.int32, (nd, na, LANE), 2)
    for c in range(3):
        own = jnp.where(wide == 8 + c, rows, 0.0)
        for k in range(FUNCS):
            base_f[c, k] = jnp.broadcast_to(one(jnp.sum(w_func[min(c, 1), k] * own, axis=0)), (SUB, LANE))

    scales = [KEEP ** k for k in range(SWEEPS)]
    depths = [min((min(nx, ny) - 1) // 2, SWEEPS - 1 - k) for k in range(SWEEPS)]

    def finish(slot, h, values):
        last = scales[SWEEPS - 1]

        def u(x, y):
            return last * h[x + 1, y] + v0[x, y]

        sums = [[], [], [], []]
        for x in range(nx):
            for side, y in ((0, ny - 1), (1, 0)):
                value = u(x, y)
                u_y[slot, side, x] = value
                sums[2 + side].append(value)
        contact = []
        for y in range(ny):
            for side, x in ((0, nx - 1), (1, 0)):
                value = u(x, y)
                u_x[slot, side, y] = value
                sums[side].append(value)
                if side:
                    contact.append(mask[y] * value)
        start_faces(slot)
        normal = jnp.where(lax.rem(slot, 3) == 0, 1.0, 0.0).astype(F32)
        post(slot, [(k, one(tree(s))) for k, s in enumerate(sums)] + [(4, normal * one(tree(contact)))])

    def first(c, carry):
        fs = [base_f[c, k] for k in range(FUNCS)]
        normal = jnp.where(c == 0, 1.0, 0.0).astype(F32)

        def fill(x, carry):
            for y in range(ny):
                value = q_ref[x, y] * load[c, x, y]
                v0[x, y] = value
                ga[x + 1, y] = value
            return carry

        lax.fori_loop(0, nx, fill, 0)
        for x, y in face_columns(nx, ny):
            f = zero
            if x == nx - 1:
                f = f + fs[0]
            if x == 0:
                f = f - fs[1] + (normal * fs[4]) * mask[y]
            if y == ny - 1:
                f = f + fs[2]
            if y == 0:
                f = f - fs[3]
            value = v0[x, y] - q_ref[x, y] * f
            v0[x, y] = value
            ga[x + 1, y] = value
        bufs = (ga, gb)
        for k in range(1, SWEEPS):
            sweep(nx, ny, depths[k], nx, bufs[(k - 1) % 2], bufs[k % 2], w_ref, 1.0 / scales[k], v0, nx,
                  k == SWEEPS - 1)
        finish(c, bufs[(SWEEPS - 1) % 2], None)
        return carry

    lax.fori_loop(0, 3, first, 0)

    def project(slot):
        wait_faces(slot)
        collect(slot)
        c = lax.rem(slot, 3)
        power = lax.div(slot, 3)
        kind = jnp.minimum(c, 1)
        sign = jnp.where(slot < 3, -1.0, 1.0).astype(F32)
        normal = jnp.where(c == 0, 1.0, 0.0).astype(F32)
        tab = table[slot]
        fs = [sign * one(jnp.sum(w_func[kind, k] * tab, axis=0)) for k in range(FUNCS)]
        fs = [jnp.broadcast_to(f, (SUB, LANE)) for f in fs]
        field, squares = {}, []

        def add(x, y, value):
            field[x, y] = value if (x, y) not in field else field[x, y] + value

        for y in range(ny):
            head = u_x[slot, 1, y]
            own = sign * (u_x[slot, 0, y] - outer * below_in[slot, y]) - fs[0]
            up = (sign * inner) * (above_in[slot, y] - head) - fs[1]
            touch = normal * mask[y] * (fs[4] - sign * head)
            y_x[slot, 0, y] = own
            y_x[slot, 1, y] = up
            y_c[slot, y] = touch
            squares += [own * own, touch * touch]
            add(nx - 1, y, own)
            add(0, y, -up - touch)
        for x in range(nx):
            own = sign * (u_y[slot, 0, x] - right_in[slot, x]) - fs[2]
            up = sign * (left_in[slot, x] - u_y[slot, 1, x]) - fs[3]
            y_y[slot, 0, x] = own
            y_y[slot, 1, x] = up
            squares.append(own * own)
            add(x, ny - 1, own)
            add(x, 0, -up)
        moments[2 * power] = moments[2 * power] + tree(squares)
        for (x, y), value in field.items():
            f_ref[x, y] = value
            value = q_ref[x, y] * value
            v0[x, y] = value
            la[x + 1, y] = value

    edge = face_columns(nx, ny)

    def krylov(i, carry):
        project(i)
        bufs = (la, lb)
        for k in range(1, SWEEPS):
            sweep(nx, ny, min(k, depths[k]), min(k - 1, SWEEPS - 1 - k + 1), bufs[(k - 1) % 2], bufs[k % 2], w_ref,
                  1.0 / scales[k], v0, 0, k == SWEEPS - 1)
        slot = i + 3
        finish(slot, bufs[(SWEEPS - 1) % 2], None)
        parts = []
        for y in range(ny):
            parts += [y_x[i, 0, y] * u_x[slot, 0, y], -(y_x[i, 1, y] + y_c[i, y]) * u_x[slot, 1, y]]
        for x in range(nx):
            parts += [y_y[i, 0, x] * u_y[slot, 0, x], -y_y[i, 1, x] * u_y[slot, 1, x]]
        odd = 2 * lax.div(i, 3) + 1
        moments[odd] = moments[odd] + tree(parts)
        return carry

    lax.fori_loop(0, 6, krylov, 0)

    def last_moment(i, carry):
        project(i)
        sweep(nx, ny, 1, 0, la, lb, w_ref, 1.0 / scales[1], v0, 0)
        sweep(nx, ny, 2, 1, lb, la, w_ref, 1.0 / scales[2], v0, 0)
        square = scales[2] * scales[2]

        acc = [zero]

        def act_on(x, lo, count, center, around):
            acc[0] = acc[0] + jnp.sum((p_ref[x, pl.ds(lo, count)] * center) * (
                (-RELAXATION * square) * center + (KEEP * square) * around), axis=0)

        region(nx, ny, 2, 2, la, w_ref, act_on)
        parts = [f_ref[x, y] * la[x + 1, y] for x, y in edge]
        moments[5] = moments[5] + acc[0] + (2.0 * scales[2]) * tree(parts)
        return carry

    lax.fori_loop(6, 9, last_moment, 0)
    post(SLOTS + 1, [(j, one(moments[j])) for j in range(6)])

    def drain(slot, c):
        faces_sent(slot)
        sent_all(slot)
        return c

    lax.fori_loop(0, SLOTS, drain, 0)
    sent_all(SLOTS)
    collect(SLOTS + 1)
    sums = jnp.sum(jnp.sum(table[SLOTS + 1], axis=0), axis=0, keepdims=True)
    m = [jnp.broadcast_to(sums[:, j : j + 1], (1, LANE)) for j in range(6)]

    a0 = m[0] / m[1]
    g1 = m[0] + 2.0 * a0 * m[1] + a0 * a0 * m[2]
    c1 = 1.0 + g1 / m[0]
    a1 = g1 / (c1 * c1 * m[1] + 2.0 * c1 * a0 * m[2] + a0 * a0 * m[3])
    pp, ss = a0 + a1 * c1, a1 * a0
    g2 = m[0] + 2.0 * pp * m[1] + (pp * pp + 2.0 * ss) * m[2] + 2.0 * pp * ss * m[3] + ss * ss * m[4]
    b2 = g2 / g1
    da, db = 1.0 + b2 * c1, pp + b2 * a0
    a2 = g2 / (da * da * m[1] + 2.0 * da * db * m[2] + (db * db + 2.0 * da * ss) * m[3]
               + 2.0 * db * ss * m[4] + ss * ss * m[5])
    k0 = jnp.broadcast_to(a0 + a1 * c1 + a2 * da, (SUB, LANE))
    k1 = jnp.broadcast_to(a1 * a0 + a2 * db, (SUB, LANE))
    k2 = jnp.broadcast_to(a2 * ss, (SUB, LANE))

    for c in range(3):
        for y in range(ny):
            res_x[c, y] = base_f[c, 0] + (k0 * y_x[c, 0, y] + k1 * y_x[3 + c, 0, y] + k2 * y_x[6 + c, 0, y])
        for x in range(nx):
            res_y[c, x] = base_f[c, 2] + (k0 * y_y[c, 0, x] + k1 * y_y[3 + c, 0, x] + k2 * y_y[6 + c, 0, x])
    for y in range(ny):
        res_c[y] = (k0 * y_c[0, y] + k1 * y_c[3, y] + k2 * y_c[6, y]) - base_f[0, 4] * mask[y]
    outputs = [pltpu.make_async_copy(a, b, out_sem.at[k])
               for k, (a, b) in enumerate(((res_x, out_x), (res_y, out_y), (res_c, out_c)))]
    for copy in outputs:
        copy.start()
    for copy in outputs:
        copy.wait()

    sent_all(SLOTS + 1)


def lay_out(in_x, in_y, in_c, out_x, out_y, out_c, sem):
    for zb in range(in_c.shape[1]):
        z = pl.ds(zb * LANE, LANE)
        pltpu.make_async_copy(in_x.at[:, :, zb, :], out_x.at[:, 0, :, z], sem.at[0]).start()
        pltpu.make_async_copy(in_y.at[:, :, zb, :], out_y.at[:, :, 0, z], sem.at[1]).start()
        pltpu.make_async_copy(in_c.at[:, zb, :], out_c.at[0, :, z], sem.at[2]).start()
    for k, ref in enumerate((in_x, in_y, in_c)):
        pltpu.make_async_copy(ref, ref, sem.at[k]).wait()


def shards(external_load, modulus, active):
    nx, ny, nz = modulus.shape
    nd, na = lax.axis_size("body"), lax.axis_size("surf")
    maps = jnp.asarray(coarse_tables(nd, na, float(ny * nz), float(nx * nz)), F32)
    tile = (SUB, LANE)
    padded, grid = (nx + 2, ny) + tile, (nx, ny) + tile
    any_spec = pl.BlockSpec(memory_space=pl.ANY)
    shapes = [
        ((3,) + grid, F32), (grid, F32), ((ny,) + tile, jnp.int32), ((FUNCS + na + 2, nd, na, LANE), F32),
        ((ny,) + tile, F32), (padded, F32), (padded, F32), ((13,) + padded, F32), (grid[:2] + (26,) + tile, F32),
        (grid, F32), (grid, F32)] + [(padded, F32)] * 4 + [
        (grid, F32), (grid, F32), ((SLOTS, 2, ny) + tile, F32), ((SLOTS, 2, nx) + tile, F32),
        ((SLOTS, ny) + tile, F32), ((SLOTS, ny) + tile, F32), ((SLOTS, nx) + tile, F32), ((SLOTS, nx) + tile, F32),
        ((SLOTS, 2, ny) + tile, F32), ((SLOTS, 2, nx) + tile, F32), ((SLOTS, ny) + tile, F32),
        ((3, FUNCS) + tile, F32), ((2, FUNCS, nd, na, LANE), F32), ((6,) + tile, F32),
        ((SLOTS + 2,) + tile, F32), ((SLOTS + 2, nd, na, LANE), F32),
        ((3, ny) + tile, F32), ((3, nx) + tile, F32), ((ny,) + tile, F32)]
    dma = pltpu.SemaphoreType.DMA
    parts = pl.pallas_call(
        functools.partial(feti_kernel, nx, ny, nz, nd, na),
        out_shape=tuple(jax.ShapeDtypeStruct(s + tile, F32) for s in ((3, ny), (3, nx), (ny,))),
        in_specs=[any_spec] * 4, out_specs=(any_spec,) * 3,
        scratch_shapes=[pltpu.VMEM(s, t) for s, t in shapes] + [
            dma((6,)), dma((3,)), dma((SLOTS, 4)), dma((SLOTS, 4)),
            dma((SLOTS + 2,)), dma((SLOTS + 2,)), dma((SLOTS + 2,))],
        compiler_params=pltpu.CompilerParams(
            vmem_limit_bytes=56 * 1024 * 1024, collective_id=0, has_side_effects=True),
    )(external_load, modulus, active, maps)
    return pl.pallas_call(
        lay_out,
        out_shape=(jax.ShapeDtypeStruct((3, 1, ny, nz), F32), jax.ShapeDtypeStruct((3, nx, 1, nz), F32),
                   jax.ShapeDtypeStruct((1, ny, nz), F32)),
        in_specs=[pl.BlockSpec(memory_space=pltpu.VMEM)] * 3, out_specs=(any_spec,) * 3, scratch_shapes=[dma((3,))],
    )(*parts)


def solution(mesh):
    placed = (P(None, "body", "surf", None), P("body", "surf", None), P("surf", None))
    return jax.shard_map(
        shards,
        mesh=mesh,
        in_specs=placed,
        out_specs=(
            P(None, "body", "surf", None),
            P(None, "body", "surf", None),
            P("body", "surf", None),
        ),
        check_vma=False,
    )
```

```python
import functools

import jax
import jax.numpy as jnp
import numpy as np
from jax import lax
from jax.experimental import pallas as pl
from jax.experimental.pallas import tpu as pltpu
from jax.sharding import PartitionSpec as P

SWEEPS = 6
COUPLING_SCALE = (0.0, 1.0, 0.5, 0.25)
RELAXATION = 0.6
KEEP = 1.0 - RELAXATION
PLANE = [(dx, dy) for dx in (-1, 0, 1) for dy in (-1, 0, 1)]
SAME = [o for o in PLANE if o != (0, 0)]
HALF = [(0, 1), (1, -1), (1, 0), (1, 1)]
SUB, LANE = 8, 128
PLUS, MINUS = 8, 17
SLOTS = 9
WIDE = 7
FUNCS = 5
F32 = jnp.float32


def shift(t, by, edge):
    axis = t.ndim - 1
    lane = lax.broadcasted_iota(jnp.int32, t.shape, axis)
    r = pltpu.roll(t, by % LANE, axis)
    return jnp.where(lane == edge, pltpu.roll(r, by % SUB, axis - 1), r)


def shift_up(t):
    return shift(t, 1, 0)


def shift_down(t):
    return shift(t, -1, LANE - 1)


def one(value):
    return jnp.sum(jnp.sum(value, axis=0, keepdims=True), axis=1, keepdims=True)


def rows_by_two(nx, act):
    def pair(i, c):
        act(2 * i)
        act(2 * i + 1)
        return c

    lax.fori_loop(0, nx // 2, pair, 0)
    if nx % 2:
        act(nx - 1)


def tree(values):
    values = list(values)
    while len(values) > 1:
        values = [a + b for a, b in zip(values[::2], values[1::2])] + (
            values[-1:] if len(values) % 2 else [])
    return values[0]


def edge_weights(nx, ny, mod, mp, ms, e_ref):
    zero = jnp.zeros((SUB, LANE), F32)
    sub = lax.broadcasted_iota(jnp.int32, (SUB, LANE), 0)
    lane = lax.broadcasted_iota(jnp.int32, (SUB, LANE), 1)
    last = (sub == SUB - 1) & (lane == LANE - 1)
    for y in range(ny):
        for ref in (mp, ms):
            ref[0, y] = zero
            ref[nx + 1, y] = zero
        for n, (dx, dy) in enumerate(HALF):
            if dx == 1:
                e_ref[n, 0, y] = zero
        for n, (dx, dy) in enumerate(PLANE):
            if dx == 1:
                e_ref[4 + n, 0, y] = zero
            if dx == -1:
                e_ref[4 + n, nx + 1, y] = zero

    def fill(x):
        for y in range(ny):
            a = mod[x, y]
            mp[x + 1, y] = a
            ms[x + 1, y] = jnp.where(last, 0.0, shift_down(a))

    rows_by_two(nx, fill)

    def row(x):
        for first, dirs, other in ((0, HALF, mp), (4, PLANE, ms)):
            for n, (dx, dy) in enumerate(dirs):
                lo, hi = max(0, -dy), ny - max(0, dy)
                a, b = mp[x + 1, pl.ds(lo, hi - lo)], other[x + 1 + dx, pl.ds(lo + dy, hi - lo)]
                scale = 2.0 * COUPLING_SCALE[abs(dx) + abs(dy) + (first > 0)]
                e_ref[first + n, x + 1, pl.ds(lo, hi - lo)] = (scale * a) * b / (a + b)

    rows_by_two(nx, row)


def same_edges(d, x, lo, count, e_ref):
    if d in HALF:
        return e_ref[HALF.index(d), x + 1, pl.ds(lo, count)]
    return e_ref[HALF.index((-d[0], -d[1])), x + 1 + d[0], pl.ds(lo + d[1], count)]


def early_edges(d, x, lo, count, e_ref):
    return e_ref[4 + PLANE.index((-d[0], -d[1])), x + 1 + d[0], pl.ds(lo + d[1], count)]


def scaled_weights(nx, ny, mp, e_ref, w_ref, q_ref, p_ref):
    sub = lax.broadcasted_iota(jnp.int32, (ny, SUB, LANE), 1)
    lane = lax.broadcasted_iota(jnp.int32, (ny, SUB, LANE), 2)
    start = (sub == 0) & (lane == 0)

    def diagonal(x):
        for lo, count in runs(range(ny), lambda y: (y == 0, y == ny - 1)):
            valid = [d for d in PLANE if 0 <= lo + d[1] and lo + count + d[1] <= ny]
            later = tree([same_edges(d, x, lo, count, e_ref) for d in valid if d != (0, 0)]
                         + [e_ref[4 + PLANE.index(d), x + 1, pl.ds(lo, count)] for d in valid])
            diag = later + shift_up(tree([early_edges(d, x, lo, count, e_ref) for d in valid]))
            q_ref[x, pl.ds(lo, count)] = RELAXATION / diag
            p_ref[x, pl.ds(lo, count)] = diag * (1.0 / RELAXATION)

    def scale(x):
        qs = q_ref[x] * (1.0 / KEEP)
        qd = shift_down(qs)
        a = jnp.where(start, 0.0, shift_up(mp[x + 1, pl.ds(0, ny)]))
        qa = shift_up(qs) * a
        for j, d in enumerate(PLANE):
            lo, hi = max(0, -d[1]), ny - max(0, d[1])
            ys = pl.ds(lo, hi - lo)
            if d != (0, 0):
                w_ref[x, ys, SAME.index(d)] = qs[lo:hi] * same_edges(d, x, lo, hi - lo, e_ref)
            b = mp[x + 1 + d[0], pl.ds(lo + d[1], hi - lo)]
            c = 2.0 * COUPLING_SCALE[abs(d[0]) + abs(d[1]) + 1]
            w_ref[x, ys, PLUS + j] = (c * qa[lo:hi]) * b / (a[lo:hi] + b)
            w_ref[x, ys, MINUS + j] = qd[lo:hi] * early_edges(d, x, lo, hi - lo, e_ref)

    rows_by_two(nx, diagonal)
    rows_by_two(nx, scale)


def to_face(x, y, nx, ny):
    return min(x, nx - 1 - x, y, ny - 1 - y)


def runs(ys, kind):
    out = []
    for y in ys:
        if out and out[-1][2] == kind(y) and out[-1][1] < WIDE:
            out[-1][1] += 1
        else:
            out.append([y, 1, kind(y)])
    return [(lo, count) for lo, count, _ in out]


def columns(x, ys, nx, ny, support, src, w_ref, act, pad=1):
    def terms(y):
        return [d for d in PLANE if 0 <= to_face(x + d[0], y + d[1], nx, ny) <= support]

    for lo, count in runs(ys, lambda y: (terms(y), to_face(x, y, nx, ny) == 0)):
        at = pl.ds(lo, count)
        mid, plus, minus, center = None, None, None, None
        for dx, dy in terms(lo):
            j = PLANE.index((dx, dy))
            value = src[x + pad + dx, pl.ds(lo + dy, count)]
            wp, wm = w_ref[x, at, PLUS + j] * value, w_ref[x, at, MINUS + j] * value
            plus = wp if plus is None else plus + wp
            minus = wm if minus is None else minus + wm
            if (dx, dy) == (0, 0):
                center = value
            else:
                w = w_ref[x, at, SAME.index((dx, dy))] * value
                mid = w if mid is None else mid + w
        act(x, lo, count, center, mid + (shift_down(plus) + shift_up(minus)))


def region(nx, ny, depth, support, src, w_ref, act, pad=1):
    for x in range(nx):
        near = min(x, nx - 1 - x) <= depth
        for ys in [range(ny)] if near else [range(0, depth + 1), range(ny - 1 - depth, ny)]:
            columns(x, ys, nx, ny, support, src, w_ref, act, pad)


def face_columns(nx, ny):
    return ([(0, y) for y in range(ny)] + [(nx - 1, y) for y in range(ny)]
            + [(x, y) for x in range(1, nx - 1) for y in (0, ny - 1)])


def sweep(nx, ny, depth, support, src, dst, w_ref, scale, v0, reach, last=False, part=None, pad=1):
    def act(x, lo, count, center, total):
        value = total if center is None else center + total
        if not last and to_face(x, lo, nx, ny) <= reach:
            value = value + scale * v0[x, pl.ds(lo, count)]
        dst[x + 1, pl.ds(lo, count)] = value

    if part is None:
        region(nx, ny, depth, support, src, w_ref, act, pad)
    else:
        for x in part[0]:
            columns(x, part[1], nx, ny, support, src, w_ref, act, pad)


def coarse_tables(nd, na, face_x, face_y):
    total = nd * na
    path = 2.0 * np.eye(nd) - np.eye(nd, k=1) - np.eye(nd, k=-1)
    path[0, 0] = 1.0
    eye = np.eye(na)
    cycle = 2.0 * eye - np.roll(eye, 1, axis=1) - np.roll(eye, -1, axis=1)
    inv = np.linalg.inv(face_x * np.kron(path, eye) + face_y * np.kron(np.eye(nd), cycle))
    ident = np.eye(total)
    up, right = np.kron(np.eye(nd, k=-1), eye), np.kron(np.eye(nd), np.roll(eye, 1, axis=0))
    part_x, part_y = ident - up, ident - right
    linked = ident.copy()
    linked[:na] = 0.0
    maps = [part_x, -part_x @ up.T, part_y, -part_y @ right.T, ident]
    out = np.zeros((nd, FUNCS + na + 2, nd, na, LANE))

    def at(b, s):
        return ident[(b * na + s % na)] if 0 <= b < nd else np.zeros(total)

    for b in range(nd):
        pick = [at(b, 0) - at(b + 1, 0), (at(b - 1, 0) - at(b, 0)) * (b > 0), at(b, 0) - at(b, 1),
                at(b, -1) - at(b, 0), at(b, 0)] + [at(0, f) for f in range(na)]
        for k, e in enumerate(pick):
            r = e @ inv
            for lane, m in enumerate(maps):
                out[b, k, :, :, lane] = (r @ m).reshape(nd, na)
            for lane in (8, 9, 10):
                out[b, k, :, :, lane] = r.reshape(nd, na)
            if k < FUNCS:
                out[b, FUNCS + na, 0, :, k] = r[:na]
        out[b, FUNCS + na + 1, 0, :, :na] = inv[:na, :na]
    return out


def feti_kernel(nx, ny, nz, nd, na, load_hbm, mod_hbm, act_hbm, maps_hbm, out_x, out_y, out_c,
                load, mod, act, maps, mask, mp, ms, e_ref, w_ref, q_ref, p_ref, ga, gb, la, lb,
                v0, f_ref, u_x, u_y, below_in, above_in, right_in, left_in,
                y_x, y_y, y_c, base_f, w_func, moments, sent, table,
                in_sem, face_send, face_recv, row_send, near_recv, far_recv):
    body, surf = lax.axis_index("body"), lax.axis_index("surf")
    total = nd * na
    below, above = lax.rem(body + 1, nd), lax.rem(body + nd - 1, nd)
    right, left = lax.rem(surf + 1, na), lax.rem(surf + na - 1, na)
    mesh_id = pl.DeviceIdType.MESH
    inner = jnp.where(body > 0, 1.0, 0.0).astype(F32)
    outer = jnp.where(body < nd - 1, 1.0, 0.0).astype(F32)
    lane = lax.broadcasted_iota(jnp.int32, (SUB, LANE), 1)
    zero = jnp.zeros((SUB, LANE), F32)
    blocks = nz // LANE
    peer_surf = [lax.rem(surf + k, na) for k in range(na)]

    def every_peer(do):
        for k in range(1, na):
            do(k, body, peer_surf[k], True)

        def others(d, c):
            there = lax.rem(body + d, nd)
            for k in range(na):
                do(k, there, peer_surf[k], False)
            return c

        lax.fori_loop(1, nd, others, 0)

    barrier = pltpu.get_barrier_semaphore()
    every_peer(lambda k, b, s, near: pl.semaphore_signal(
        barrier, inc=1, device_id=(b, s), device_id_type=mesh_id))

    for zb in range(blocks):
        z = pl.ds(zb * LANE, LANE)
        pltpu.make_async_copy(mod_hbm.at[:, :, z], mod.at[:, :, zb, :], in_sem.at[1]).start()
    for zb in range(blocks):
        z = pl.ds(zb * LANE, LANE)
        for c in range(3):
            pltpu.make_async_copy(load_hbm.at[c, :, :, z], load.at[c, :, :, zb, :], in_sem.at[3 + c]).start()
        pltpu.make_async_copy(act_hbm.at[:, z], act.at[:, zb, :], in_sem.at[0]).start()
    maps_copy = pltpu.make_async_copy(maps_hbm.at[body], maps, in_sem.at[2])
    maps_copy.start()

    def post(slot, values):
        row = jnp.zeros((SUB, LANE), F32)
        for k, value in values:
            row = jnp.where(lane == k, value, row)
        sent[slot] = row
        table[slot, body, pl.ds(0, 1)] = row[0:1]

        def send(k, b, s, near):
            pltpu.make_async_remote_copy(
                src_ref=sent.at[slot, pl.ds(0, 1)], dst_ref=table.at[slot, body, pl.ds((na - k) % na, 1)],
                send_sem=row_send.at[slot], recv_sem=(near_recv if near else far_recv).at[slot],
                device_id=(b, s), device_id_type=mesh_id).start()

        every_peer(send)

    def row_wait(slot, ref, sem):
        return pltpu.make_async_remote_copy(
            src_ref=ref, dst_ref=ref, send_sem=row_send.at[slot], recv_sem=sem.at[slot],
            device_id=(body, right), device_id_type=mesh_id)

    def collect(slot):
        row_wait(slot, table.at[slot, 0, pl.ds(0, na - 1)], near_recv).wait_recv()
        row_wait(slot, table.at[slot, pl.ds(0, nd - 1)], far_recv).wait_recv()

    def sent_all(slot):
        row_wait(slot, table.at[slot, 0, pl.ds(0, na - 1)], near_recv).wait_send()
        row_wait(slot, table.at[slot, pl.ds(0, nd - 1)], far_recv).wait_send()

    def faces(slot):
        def copy(i, src, dst, peer):
            return pltpu.make_async_remote_copy(
                src_ref=src, dst_ref=dst, send_sem=face_send.at[slot, i], recv_sem=face_recv.at[slot, i],
                device_id=peer, device_id_type=mesh_id)

        return (copy(0, u_y.at[slot, 1], right_in.at[slot], (body, left)),
                copy(1, u_y.at[slot, 0], left_in.at[slot], (body, right)),
                copy(2, u_x.at[slot, 1], below_in.at[slot], (above, surf)),
                copy(3, u_x.at[slot, 0], above_in.at[slot], (below, surf)))

    def start_faces(slot):
        to_left, to_right, to_above, to_below = faces(slot)
        to_left.start()
        to_right.start()
        pl.when(body > 0)(to_above.start)
        pl.when(body < nd - 1)(to_below.start)

    def wait_faces(slot):
        to_left, to_right, to_above, to_below = faces(slot)
        to_left.wait_recv()
        to_right.wait_recv()
        pl.when(body < nd - 1)(to_above.wait_recv)
        pl.when(body > 0)(to_below.wait_recv)

    def faces_sent(slot):
        to_left, to_right, to_above, to_below = faces(slot)
        to_left.wait_send()
        to_right.wait_send()
        pl.when(body > 0)(to_above.wait_send)
        pl.when(body < nd - 1)(to_below.wait_send)

    def arrived(ref, sem):
        pltpu.make_async_copy(ref, ref, in_sem.at[sem]).wait()

    arrived(mod, 1)
    edge_weights(nx, ny, mod, mp, ms, e_ref)
    for c in range(3):
        arrived(load.at[c], 3 + c)
    arrived(act, 0)
    top = jnp.where(body == 0, 1.0, 0.0).astype(F32)
    count = zero
    for y in range(ny):
        mask[y] = act[y].astype(F32) * top
        count = count + mask[y]

    def load_row(x, sums):
        return tuple(s + tree([load[c, x, y] for y in range(ny)]) for c, s in enumerate(sums))

    load_sums = lax.fori_loop(0, nx, load_row, (zero,) * 3)
    pl.semaphore_wait(barrier, total - 1)
    post(SLOTS, [(8 + c, one(load_sums[c])) for c in range(3)] + [(11, one(count))])
    @pl.when(body == 0)
    def _():
        above_in[...] = jnp.zeros_like(above_in)

    @pl.when(body == nd - 1)
    def _():
        below_in[...] = jnp.zeros_like(below_in)

    scaled_weights(nx, ny, mp, e_ref, w_ref, q_ref, p_ref)

    scales = [KEEP ** k for k in range(SWEEPS)]
    depths = [min((min(nx, ny) - 1) // 2, SWEEPS - 1 - k) for k in range(SWEEPS)]

    moments[...] = jnp.zeros_like(moments)

    def inside(c, carry):
        def row(x, carry):
            load[c, x] = q_ref[x] * load[c, x]
            return carry

        lax.fori_loop(0, nx, row, 0)
        sweep(nx, ny, nx, nx, load.at[c], gb.at[c], w_ref, 1.0 / scales[1], load.at[c], nx,
              part=(range(2, nx - 2), range(2, ny - 2)), pad=0)
        return carry

    lax.fori_loop(0, 3, inside, 0)
    maps_copy.wait()
    collect(SLOTS)

    rows = table[SLOTS]
    counts = jnp.sum(jnp.where(lax.broadcasted_iota(jnp.int32, (na, LANE), 1) == 11, rows[0], 0.0),
                     axis=1, keepdims=True)
    sq_row = lax.broadcasted_iota(jnp.int32, (na, LANE), 0)
    sq_col = lax.broadcasted_iota(jnp.int32, (na, LANE), 1)
    work = jnp.where(sq_row == sq_col, 1.0, 0.0) + counts * maps[FUNCS + na + 1, 0]
    other = counts * maps[FUNCS + na, 0]
    row_id = lax.broadcasted_iota(jnp.int32, (na, 1), 0)
    for k in range(na):
        scale = 1.0 / work[k : k + 1, k : k + 1]
        pivot, tail = work[k : k + 1] * scale, other[k : k + 1] * scale
        factor = work[:, k : k + 1]
        work = jnp.where(row_id == k, pivot, work - factor * pivot)
        other = jnp.where(row_id == k, tail, other - factor * tail)
    for k in range(FUNCS):
        plain = maps[k]
        w_func[1, k] = plain
        w_func[0, k] = plain - tree([other[f : f + 1, k : k + 1] * maps[FUNCS + f] for f in range(na)])

    wide = lax.broadcasted_iota(jnp.int32, (nd, na, LANE), 2)
    for c in range(3):
        own = jnp.where(wide == 8 + c, rows, 0.0)
        for k in range(FUNCS):
            base_f[c, k] = jnp.broadcast_to(one(jnp.sum(w_func[min(c, 1), k] * own, axis=0)), (SUB, LANE))

    def finish(slot, h, v0):
        last = scales[SWEEPS - 1]

        def u(x, y):
            return last * h[x + 1, y] + v0[x, y]

        sums = [[], [], [], []]
        for x in range(nx):
            for side, y in ((0, ny - 1), (1, 0)):
                value = u(x, y)
                u_y[slot, side, x] = value
                sums[2 + side].append(value)
        contact = []
        for y in range(ny):
            for side, x in ((0, nx - 1), (1, 0)):
                value = u(x, y)
                u_x[slot, side, y] = value
                sums[side].append(value)
                if side:
                    contact.append(mask[y] * value)
        start_faces(slot)
        normal = jnp.where(lax.rem(slot, 3) == 0, 1.0, 0.0).astype(F32)
        post(slot, [(k, one(tree(s))) for k, s in enumerate(sums)] + [(4, normal * one(tree(contact)))])

    def first(c, carry):
        fs = [base_f[c, k] for k in range(FUNCS)]
        normal = jnp.where(c == 0, 1.0, 0.0).astype(F32)

        source = load.at[c]
        for x, y in face_columns(nx, ny):
            f = zero
            if x == nx - 1:
                f = f + fs[0]
            if x == 0:
                f = f - fs[1] + (normal * fs[4]) * mask[y]
            if y == ny - 1:
                f = f + fs[2]
            if y == 0:
                f = f - fs[3]
            source[x, y] = source[x, y] - q_ref[x, y] * f
        sweep(nx, ny, 1, nx, source, gb.at[c], w_ref, 1.0 / scales[1], source, nx, pad=0)
        bufs = (ga, gb.at[c])
        for k in range(2, SWEEPS):
            sweep(nx, ny, depths[k], nx, bufs[(k - 1) % 2], bufs[k % 2], w_ref, 1.0 / scales[k], source, nx,
                  k == SWEEPS - 1)
        finish(c, bufs[(SWEEPS - 1) % 2], source)
        return carry

    lax.fori_loop(0, 3, first, 0)

    def project(slot):
        wait_faces(slot)
        collect(slot)
        c = lax.rem(slot, 3)
        power = lax.div(slot, 3)
        kind = jnp.minimum(c, 1)
        sign = jnp.where(slot < 3, -1.0, 1.0).astype(F32)
        normal = jnp.where(c == 0, 1.0, 0.0).astype(F32)
        tab = table[slot]
        fs = [sign * one(jnp.sum(w_func[kind, k] * tab, axis=0)) for k in range(FUNCS)]
        fs = [jnp.broadcast_to(f, (SUB, LANE)) for f in fs]
        field, squares = {}, []

        def add(x, y, value):
            field[x, y] = value if (x, y) not in field else field[x, y] + value

        for y in range(ny):
            head = u_x[slot, 1, y]
            own = sign * (u_x[slot, 0, y] - outer * below_in[slot, y]) - fs[0]
            up = (sign * inner) * (above_in[slot, y] - head) - fs[1]
            touch = normal * mask[y] * (fs[4] - sign * head)
            y_x[slot, 0, y] = own
            y_x[slot, 1, y] = up
            y_c[slot, y] = touch
            squares += [own * own, touch * touch]
            add(nx - 1, y, own)
            add(0, y, -up - touch)
        for x in range(nx):
            own = sign * (u_y[slot, 0, x] - right_in[slot, x]) - fs[2]
            up = sign * (left_in[slot, x] - u_y[slot, 1, x]) - fs[3]
            y_y[slot, 0, x] = own
            y_y[slot, 1, x] = up
            squares.append(own * own)
            add(x, ny - 1, own)
            add(x, 0, -up)
        moments[2 * power] = moments[2 * power] + tree(squares)
        for (x, y), value in field.items():
            f_ref[x, y] = value
            value = q_ref[x, y] * value
            v0[x, y] = value
            la[x + 1, y] = value

    edge = face_columns(nx, ny)

    def krylov(i, carry):
        project(i)
        bufs = (la, lb)
        for k in range(1, SWEEPS):
            sweep(nx, ny, min(k, depths[k]), min(k - 1, SWEEPS - 1 - k + 1), bufs[(k - 1) % 2], bufs[k % 2], w_ref,
                  1.0 / scales[k], v0, 0, k == SWEEPS - 1)
        slot = i + 3
        finish(slot, bufs[(SWEEPS - 1) % 2], v0)
        parts = []
        for y in range(ny):
            parts += [y_x[i, 0, y] * u_x[slot, 0, y], -(y_x[i, 1, y] + y_c[i, y]) * u_x[slot, 1, y]]
        for x in range(nx):
            parts += [y_y[i, 0, x] * u_y[slot, 0, x], -y_y[i, 1, x] * u_y[slot, 1, x]]
        odd = 2 * lax.div(i, 3) + 1
        moments[odd] = moments[odd] + tree(parts)
        return carry

    lax.fori_loop(0, 6, krylov, 0)

    def last_moment(i, carry):
        project(i)
        sweep(nx, ny, 1, 0, la, lb, w_ref, 1.0 / scales[1], v0, 0)
        sweep(nx, ny, 2, 1, lb, la, w_ref, 1.0 / scales[2], v0, 0)
        square = scales[2] * scales[2]

        acc = [zero]

        def act_on(x, lo, count, center, around):
            acc[0] = acc[0] + jnp.sum((p_ref[x, pl.ds(lo, count)] * center) * (
                (-RELAXATION * square) * center + (KEEP * square) * around), axis=0)

        region(nx, ny, 2, 2, la, w_ref, act_on)
        parts = [f_ref[x, y] * la[x + 1, y] for x, y in edge]
        moments[5] = moments[5] + acc[0] + (2.0 * scales[2]) * tree(parts)
        return carry

    lax.fori_loop(6, 9, last_moment, 0)
    post(SLOTS + 1, [(j, one(moments[j])) for j in range(6)])

    def drain(slot, c):
        faces_sent(slot)
        sent_all(slot)
        return c

    lax.fori_loop(0, SLOTS, drain, 0)
    sent_all(SLOTS)
    collect(SLOTS + 1)
    sums = jnp.sum(jnp.sum(table[SLOTS + 1], axis=0), axis=0, keepdims=True)
    m = [jnp.broadcast_to(sums[:, j : j + 1], (1, LANE)) for j in range(6)]

    a0 = m[0] / m[1]
    g1 = m[0] + 2.0 * a0 * m[1] + a0 * a0 * m[2]
    c1 = 1.0 + g1 / m[0]
    a1 = g1 / (c1 * c1 * m[1] + 2.0 * c1 * a0 * m[2] + a0 * a0 * m[3])
    pp, ss = a0 + a1 * c1, a1 * a0
    g2 = m[0] + 2.0 * pp * m[1] + (pp * pp + 2.0 * ss) * m[2] + 2.0 * pp * ss * m[3] + ss * ss * m[4]
    b2 = g2 / g1
    da, db = 1.0 + b2 * c1, pp + b2 * a0
    a2 = g2 / (da * da * m[1] + 2.0 * da * db * m[2] + (db * db + 2.0 * da * ss) * m[3]
               + 2.0 * db * ss * m[4] + ss * ss * m[5])
    k0 = jnp.broadcast_to(a0 + a1 * c1 + a2 * da, (SUB, LANE))
    k1 = jnp.broadcast_to(a1 * a0 + a2 * db, (SUB, LANE))
    k2 = jnp.broadcast_to(a2 * ss, (SUB, LANE))

    for c in range(3):
        for y in range(ny):
            out_x[c, y] = base_f[c, 0] + (k0 * y_x[c, 0, y] + k1 * y_x[3 + c, 0, y] + k2 * y_x[6 + c, 0, y])
        for x in range(nx):
            out_y[c, x] = base_f[c, 2] + (k0 * y_y[c, 0, x] + k1 * y_y[3 + c, 0, x] + k2 * y_y[6 + c, 0, x])
    for y in range(ny):
        out_c[y] = (k0 * y_c[0, y] + k1 * y_c[3, y] + k2 * y_c[6, y]) - base_f[0, 4] * mask[y]

    sent_all(SLOTS + 1)


def lay_out(in_x, in_y, in_c, out_x, out_y, out_c, sem):
    for zb in range(in_c.shape[1]):
        z = pl.ds(zb * LANE, LANE)
        pltpu.make_async_copy(in_x.at[:, :, zb, :], out_x.at[:, 0, :, z], sem.at[0]).start()
        pltpu.make_async_copy(in_y.at[:, :, zb, :], out_y.at[:, :, 0, z], sem.at[1]).start()
        pltpu.make_async_copy(in_c.at[:, zb, :], out_c.at[0, :, z], sem.at[2]).start()
    for k, ref in enumerate((in_x, in_y, in_c)):
        pltpu.make_async_copy(ref, ref, sem.at[k]).wait()


def shards(external_load, modulus, active):
    nx, ny, nz = modulus.shape
    nd, na = lax.axis_size("body"), lax.axis_size("surf")
    maps = jnp.asarray(coarse_tables(nd, na, float(ny * nz), float(nx * nz)), F32)
    tile = (SUB, LANE)
    padded, grid = (nx + 2, ny) + tile, (nx, ny) + tile
    any_spec = pl.BlockSpec(memory_space=pl.ANY)
    shapes = [
        ((3,) + grid, F32), (grid, F32), ((ny,) + tile, jnp.int32), ((FUNCS + na + 2, nd, na, LANE), F32),
        ((ny,) + tile, F32), (padded, F32), (padded, F32), ((13,) + padded, F32), (grid[:2] + (26,) + tile, F32),
        (grid, F32), (grid, F32)] + [(padded, F32), ((3,) + padded, F32), (padded, F32), (padded, F32)] + [
        (grid, F32), (grid, F32), ((SLOTS, 2, ny) + tile, F32), ((SLOTS, 2, nx) + tile, F32),
        ((SLOTS, ny) + tile, F32), ((SLOTS, ny) + tile, F32), ((SLOTS, nx) + tile, F32), ((SLOTS, nx) + tile, F32),
        ((SLOTS, 2, ny) + tile, F32), ((SLOTS, 2, nx) + tile, F32), ((SLOTS, ny) + tile, F32),
        ((3, FUNCS) + tile, F32), ((2, FUNCS, nd, na, LANE), F32), ((6,) + tile, F32),
        ((SLOTS + 2,) + tile, F32), ((SLOTS + 2, nd, na, LANE), F32)]
    dma = pltpu.SemaphoreType.DMA
    parts = pl.pallas_call(
        functools.partial(feti_kernel, nx, ny, nz, nd, na),
        out_shape=tuple(jax.ShapeDtypeStruct(s + tile, F32) for s in ((3, ny), (3, nx), (ny,))),
        in_specs=[pl.BlockSpec(memory_space=pltpu.HBM)] * 4, out_specs=(pl.BlockSpec(memory_space=pltpu.VMEM),) * 3,
        scratch_shapes=[pltpu.VMEM(s, t) for s, t in shapes] + [
            dma((6,)), dma((SLOTS, 4)), dma((SLOTS, 4)),
            dma((SLOTS + 2,)), dma((SLOTS + 2,)), dma((SLOTS + 2,))],
        compiler_params=pltpu.CompilerParams(
            vmem_limit_bytes=54700 * 1024, collective_id=0, has_side_effects=True),
    )(external_load, modulus, active, maps)
    return pl.pallas_call(
        lay_out,
        out_shape=(jax.ShapeDtypeStruct((3, 1, ny, nz), F32), jax.ShapeDtypeStruct((3, nx, 1, nz), F32),
                   jax.ShapeDtypeStruct((1, ny, nz), F32)),
        in_specs=[any_spec] * 3, out_specs=(any_spec,) * 3, scratch_shapes=[dma((3,))],
        compiler_params=pltpu.CompilerParams(vmem_limit_bytes=4 * 1024 * 1024),
    )(*parts)


def solution(mesh):
    placed = (P(None, "body", "surf", None), P("body", "surf", None), P("surf", None))
    return jax.shard_map(
        shards,
        mesh=mesh,
        in_specs=placed,
        out_specs=(
            P(None, "body", "surf", None),
            P(None, "body", "surf", None),
            P("body", "surf", None),
        ),
        check_vma=False,
    )
```

```python
import functools

import jax
import jax.numpy as jnp
import numpy as np
from jax import lax
from jax.experimental import pallas as pl
from jax.experimental.pallas import tpu as pltpu
from jax.sharding import PartitionSpec as P

SWEEPS = 6
COUPLING_SCALE = (0.0, 1.0, 0.5, 0.25)
RELAXATION = 0.6
KEEP = 1.0 - RELAXATION
PLANE = [(dx, dy) for dx in (-1, 0, 1) for dy in (-1, 0, 1)]
SAME = [o for o in PLANE if o != (0, 0)]
HALF = [(0, 1), (1, -1), (1, 0), (1, 1)]
SUB, LANE = 8, 128
PLUS, MINUS = 8, 17
SLOTS = 9
WIDE = 7
FUNCS = 5
F32 = jnp.float32


def shift(t, by, edge):
    axis = t.ndim - 1
    lane = lax.broadcasted_iota(jnp.int32, t.shape, axis)
    r = pltpu.roll(t, by % LANE, axis)
    return jnp.where(lane == edge, pltpu.roll(r, by % SUB, axis - 1), r)


def shift_up(t):
    return shift(t, 1, 0)


def shift_down(t):
    return shift(t, -1, LANE - 1)


def one(value):
    return jnp.sum(jnp.sum(value, axis=0, keepdims=True), axis=1, keepdims=True)


def rows_by_two(nx, act):
    def pair(i, c):
        act(2 * i)
        act(2 * i + 1)
        return c

    lax.fori_loop(0, nx // 2, pair, 0)
    if nx % 2:
        act(nx - 1)


def tree(values):
    values = list(values)
    while len(values) > 1:
        values = [a + b for a, b in zip(values[::2], values[1::2])] + (
            values[-1:] if len(values) % 2 else [])
    return values[0]


def edge_weights(nx, ny, mod, mp, ms, e_ref):
    zero = jnp.zeros((SUB, LANE), F32)
    sub = lax.broadcasted_iota(jnp.int32, (SUB, LANE), 0)
    lane = lax.broadcasted_iota(jnp.int32, (SUB, LANE), 1)
    last = (sub == SUB - 1) & (lane == LANE - 1)
    for y in range(ny):
        for ref in (mp, ms):
            ref[0, y] = zero
            ref[nx + 1, y] = zero
        for n, (dx, dy) in enumerate(HALF):
            if dx == 1:
                e_ref[n, 0, y] = zero
        for n, (dx, dy) in enumerate(PLANE):
            if dx == 1:
                e_ref[4 + n, 0, y] = zero
            if dx == -1:
                e_ref[4 + n, nx + 1, y] = zero

    def fill(x):
        for y in range(ny):
            a = mod[x, y]
            mp[x + 1, y] = a
            ms[x + 1, y] = jnp.where(last, 0.0, shift_down(a))

    rows_by_two(nx, fill)

    def row(x):
        for first, dirs, other in ((0, HALF, mp), (4, PLANE, ms)):
            for n, (dx, dy) in enumerate(dirs):
                lo, hi = max(0, -dy), ny - max(0, dy)
                a, b = mp[x + 1, pl.ds(lo, hi - lo)], other[x + 1 + dx, pl.ds(lo + dy, hi - lo)]
                scale = 2.0 * COUPLING_SCALE[abs(dx) + abs(dy) + (first > 0)]
                e_ref[first + n, x + 1, pl.ds(lo, hi - lo)] = (scale * a) * b / (a + b)

    rows_by_two(nx, row)


def same_edges(d, x, lo, count, e_ref):
    if d in HALF:
        return e_ref[HALF.index(d), x + 1, pl.ds(lo, count)]
    return e_ref[HALF.index((-d[0], -d[1])), x + 1 + d[0], pl.ds(lo + d[1], count)]


def early_edges(d, x, lo, count, e_ref):
    return e_ref[4 + PLANE.index((-d[0], -d[1])), x + 1 + d[0], pl.ds(lo + d[1], count)]


def scaled_weights(nx, ny, mp, e_ref, w_ref, q_ref, p_ref):
    sub = lax.broadcasted_iota(jnp.int32, (ny, SUB, LANE), 1)
    lane = lax.broadcasted_iota(jnp.int32, (ny, SUB, LANE), 2)
    start = (sub == 0) & (lane == 0)

    def diagonal(x):
        for lo, count in runs(range(ny), lambda y: (y == 0, y == ny - 1)):
            valid = [d for d in PLANE if 0 <= lo + d[1] and lo + count + d[1] <= ny]
            later = tree([same_edges(d, x, lo, count, e_ref) for d in valid if d != (0, 0)]
                         + [e_ref[4 + PLANE.index(d), x + 1, pl.ds(lo, count)] for d in valid])
            diag = later + shift_up(tree([early_edges(d, x, lo, count, e_ref) for d in valid]))
            q_ref[x, pl.ds(lo, count)] = RELAXATION / diag
            p_ref[x, pl.ds(lo, count)] = diag * (1.0 / RELAXATION)

    def scale(x):
        qs = q_ref[x] * (1.0 / KEEP)
        qd = shift_down(qs)
        a = jnp.where(start, 0.0, shift_up(mp[x + 1, pl.ds(0, ny)]))
        qa = shift_up(qs) * a
        for j, d in enumerate(PLANE):
            lo, hi = max(0, -d[1]), ny - max(0, d[1])
            ys = pl.ds(lo, hi - lo)
            if d != (0, 0):
                w_ref[x, ys, SAME.index(d)] = qs[lo:hi] * same_edges(d, x, lo, hi - lo, e_ref)
            b = mp[x + 1 + d[0], pl.ds(lo + d[1], hi - lo)]
            c = 2.0 * COUPLING_SCALE[abs(d[0]) + abs(d[1]) + 1]
            w_ref[x, ys, PLUS + j] = (c * qa[lo:hi]) * b / (a[lo:hi] + b)
            w_ref[x, ys, MINUS + j] = qd[lo:hi] * early_edges(d, x, lo, hi - lo, e_ref)

    rows_by_two(nx, diagonal)
    rows_by_two(nx, scale)


def to_face(x, y, nx, ny):
    return min(x, nx - 1 - x, y, ny - 1 - y)


def runs(ys, kind):
    out = []
    for y in ys:
        if out and out[-1][2] == kind(y) and out[-1][1] < WIDE:
            out[-1][1] += 1
        else:
            out.append([y, 1, kind(y)])
    return [(lo, count) for lo, count, _ in out]


def columns(x, ys, nx, ny, support, src, w_ref, act, pad=1):
    def terms(y):
        return [d for d in PLANE if 0 <= to_face(x + d[0], y + d[1], nx, ny) <= support]

    for lo, count in runs(ys, lambda y: (terms(y), to_face(x, y, nx, ny) == 0)):
        at = pl.ds(lo, count)
        mid, plus, minus, center = None, None, None, None
        for dx, dy in terms(lo):
            j = PLANE.index((dx, dy))
            value = src[x + pad + dx, pl.ds(lo + dy, count)]
            wp, wm = w_ref[x, at, PLUS + j] * value, w_ref[x, at, MINUS + j] * value
            plus = wp if plus is None else plus + wp
            minus = wm if minus is None else minus + wm
            if (dx, dy) == (0, 0):
                center = value
            else:
                w = w_ref[x, at, SAME.index((dx, dy))] * value
                mid = w if mid is None else mid + w
        act(x, lo, count, center, mid + (shift_down(plus) + shift_up(minus)))


def region(nx, ny, depth, support, src, w_ref, act, pad=1):
    for x in range(nx):
        near = min(x, nx - 1 - x) <= depth
        for ys in [range(ny)] if near else [range(0, depth + 1), range(ny - 1 - depth, ny)]:
            columns(x, ys, nx, ny, support, src, w_ref, act, pad)


def face_columns(nx, ny):
    return ([(0, y) for y in range(ny)] + [(nx - 1, y) for y in range(ny)]
            + [(x, y) for x in range(1, nx - 1) for y in (0, ny - 1)])


def sweep(nx, ny, depth, support, src, dst, w_ref, scale, v0, reach, last=False, part=None, pad=1):
    def act(x, lo, count, center, total):
        value = total if center is None else center + total
        if not last and to_face(x, lo, nx, ny) <= reach:
            value = value + scale * v0[x, pl.ds(lo, count)]
        dst[x + 1, pl.ds(lo, count)] = value

    if part is None:
        region(nx, ny, depth, support, src, w_ref, act, pad)
    else:
        for x in part[0]:
            columns(x, part[1], nx, ny, support, src, w_ref, act, pad)


def coarse_tables(nd, na, face_x, face_y):
    total = nd * na
    path = 2.0 * np.eye(nd) - np.eye(nd, k=1) - np.eye(nd, k=-1)
    path[0, 0] = 1.0
    eye = np.eye(na)
    cycle = 2.0 * eye - np.roll(eye, 1, axis=1) - np.roll(eye, -1, axis=1)
    inv = np.linalg.inv(face_x * np.kron(path, eye) + face_y * np.kron(np.eye(nd), cycle))
    ident = np.eye(total)
    up, right = np.kron(np.eye(nd, k=-1), eye), np.kron(np.eye(nd), np.roll(eye, 1, axis=0))
    part_x, part_y = ident - up, ident - right
    linked = ident.copy()
    linked[:na] = 0.0
    maps = [part_x, -part_x @ up.T, part_y, -part_y @ right.T, ident]
    out = np.zeros((nd, FUNCS + na + 2, nd, na, LANE))

    def at(b, s):
        return ident[(b * na + s % na)] if 0 <= b < nd else np.zeros(total)

    for b in range(nd):
        pick = [at(b, 0) - at(b + 1, 0), (at(b - 1, 0) - at(b, 0)) * (b > 0), at(b, 0) - at(b, 1),
                at(b, -1) - at(b, 0), at(b, 0)] + [at(0, f) for f in range(na)]
        for k, e in enumerate(pick):
            r = e @ inv
            for lane, m in enumerate(maps):
                out[b, k, :, :, lane] = (r @ m).reshape(nd, na)
            for lane in (8, 9, 10):
                out[b, k, :, :, lane] = r.reshape(nd, na)
            if k < FUNCS:
                out[b, FUNCS + na, 0, :, k] = r[:na]
        out[b, FUNCS + na + 1, 0, :, :na] = inv[:na, :na]
    return out


def feti_kernel(nx, ny, nz, nd, na, load_hbm, mod_hbm, act_hbm, maps_hbm, out_x, out_y, out_c,
                load, mod, act, maps, mask, mp, ms, e_ref, w_ref, q_ref, p_ref, ga, gb, la, lb,
                v0, f_ref, u_x, u_y, below_in, above_in, right_in, left_in,
                y_x, y_y, y_c, base_f, f_next, w_func, moments, sent, table,
                in_sem, face_send, face_recv, row_send, near_recv, far_recv):
    body, surf = lax.axis_index("body"), lax.axis_index("surf")
    total = nd * na
    below, above = lax.rem(body + 1, nd), lax.rem(body + nd - 1, nd)
    right, left = lax.rem(surf + 1, na), lax.rem(surf + na - 1, na)
    mesh_id = pl.DeviceIdType.MESH
    inner = jnp.where(body > 0, 1.0, 0.0).astype(F32)
    outer = jnp.where(body < nd - 1, 1.0, 0.0).astype(F32)
    lane = lax.broadcasted_iota(jnp.int32, (SUB, LANE), 1)
    zero = jnp.zeros((SUB, LANE), F32)
    blocks = nz // LANE
    peer_surf = [lax.rem(surf + k, na) for k in range(na)]

    def every_peer(do):
        for k in range(1, na):
            do(k, body, peer_surf[k], True)

        def others(d, c):
            there = lax.rem(body + d, nd)
            for k in range(na):
                do(k, there, peer_surf[k], False)
            return c

        lax.fori_loop(1, nd, others, 0)

    barrier = pltpu.get_barrier_semaphore()
    every_peer(lambda k, b, s, near: pl.semaphore_signal(
        barrier, inc=1, device_id=(b, s), device_id_type=mesh_id))

    for zb in range(blocks):
        z = pl.ds(zb * LANE, LANE)
        pltpu.make_async_copy(mod_hbm.at[:, :, z], mod.at[:, :, zb, :], in_sem.at[1]).start()
    for zb in range(blocks):
        z = pl.ds(zb * LANE, LANE)
        for c in range(3):
            pltpu.make_async_copy(load_hbm.at[c, :, :, z], load.at[c, :, :, zb, :], in_sem.at[3 + c]).start()
        pltpu.make_async_copy(act_hbm.at[:, z], act.at[:, zb, :], in_sem.at[0]).start()
    maps_copy = pltpu.make_async_copy(maps_hbm.at[body], maps, in_sem.at[2])
    maps_copy.start()

    def post(slot, values):
        row = jnp.zeros((SUB, LANE), F32)
        for k, value in values:
            row = jnp.where(lane == k, value, row)
        sent[slot] = row
        table[slot, body, pl.ds(0, 1)] = row[0:1]

        def send(k, b, s, near):
            pltpu.make_async_remote_copy(
                src_ref=sent.at[slot, pl.ds(0, 1)], dst_ref=table.at[slot, body, pl.ds((na - k) % na, 1)],
                send_sem=row_send.at[slot], recv_sem=(near_recv if near else far_recv).at[slot],
                device_id=(b, s), device_id_type=mesh_id).start()

        every_peer(send)

    def row_wait(slot, ref, sem):
        return pltpu.make_async_remote_copy(
            src_ref=ref, dst_ref=ref, send_sem=row_send.at[slot], recv_sem=sem.at[slot],
            device_id=(body, right), device_id_type=mesh_id)

    def collect(slot):
        row_wait(slot, table.at[slot, 0, pl.ds(0, na - 1)], near_recv).wait_recv()
        row_wait(slot, table.at[slot, pl.ds(0, nd - 1)], far_recv).wait_recv()

    def sent_all(slot):
        row_wait(slot, table.at[slot, 0, pl.ds(0, na - 1)], near_recv).wait_send()
        row_wait(slot, table.at[slot, pl.ds(0, nd - 1)], far_recv).wait_send()

    def faces(slot):
        def copy(i, src, dst, peer):
            return pltpu.make_async_remote_copy(
                src_ref=src, dst_ref=dst, send_sem=face_send.at[slot, i], recv_sem=face_recv.at[slot, i],
                device_id=peer, device_id_type=mesh_id)

        return (copy(0, u_y.at[slot, 1], right_in.at[slot], (body, left)),
                copy(1, u_y.at[slot, 0], left_in.at[slot], (body, right)),
                copy(2, u_x.at[slot, 1], below_in.at[slot], (above, surf)),
                copy(3, u_x.at[slot, 0], above_in.at[slot], (below, surf)))

    def start_faces(slot):
        to_left, to_right, to_above, to_below = faces(slot)
        to_left.start()
        to_right.start()
        pl.when(body > 0)(to_above.start)
        pl.when(body < nd - 1)(to_below.start)

    def wait_faces(slot):
        to_left, to_right, to_above, to_below = faces(slot)
        to_left.wait_recv()
        to_right.wait_recv()
        pl.when(body < nd - 1)(to_above.wait_recv)
        pl.when(body > 0)(to_below.wait_recv)

    def faces_sent(slot):
        to_left, to_right, to_above, to_below = faces(slot)
        to_left.wait_send()
        to_right.wait_send()
        pl.when(body > 0)(to_above.wait_send)
        pl.when(body < nd - 1)(to_below.wait_send)

    def arrived(ref, sem):
        pltpu.make_async_copy(ref, ref, in_sem.at[sem]).wait()

    arrived(mod, 1)
    edge_weights(nx, ny, mod, mp, ms, e_ref)
    for c in range(3):
        arrived(load.at[c], 3 + c)
    arrived(act, 0)
    top = jnp.where(body == 0, 1.0, 0.0).astype(F32)
    count = zero
    for y in range(ny):
        mask[y] = act[y].astype(F32) * top
        count = count + mask[y]

    def load_row(x, sums):
        return tuple(s + tree([load[c, x, y] for y in range(ny)]) for c, s in enumerate(sums))

    load_sums = lax.fori_loop(0, nx, load_row, (zero,) * 3)
    pl.semaphore_wait(barrier, total - 1)
    post(SLOTS, [(8 + c, one(load_sums[c])) for c in range(3)] + [(11, one(count))])
    @pl.when(body == 0)
    def _():
        above_in[...] = jnp.zeros_like(above_in)

    @pl.when(body == nd - 1)
    def _():
        below_in[...] = jnp.zeros_like(below_in)

    scaled_weights(nx, ny, mp, e_ref, w_ref, q_ref, p_ref)

    scales = [KEEP ** k for k in range(SWEEPS)]
    depths = [min((min(nx, ny) - 1) // 2, SWEEPS - 1 - k) for k in range(SWEEPS)]

    moments[...] = jnp.zeros_like(moments)

    def inside(c, carry):
        def row(x, carry):
            load[c, x] = q_ref[x] * load[c, x]
            return carry

        lax.fori_loop(0, nx, row, 0)
        sweep(nx, ny, nx, nx, load.at[c], gb.at[c], w_ref, 1.0 / scales[1], load.at[c], nx,
              part=(range(2, nx - 2), range(2, ny - 2)), pad=0)
        return carry

    lax.fori_loop(0, 3, inside, 0)
    maps_copy.wait()
    collect(SLOTS)

    rows = table[SLOTS]
    counts = jnp.sum(jnp.where(lax.broadcasted_iota(jnp.int32, (na, LANE), 1) == 11, rows[0], 0.0),
                     axis=1, keepdims=True)
    sq_row = lax.broadcasted_iota(jnp.int32, (na, LANE), 0)
    sq_col = lax.broadcasted_iota(jnp.int32, (na, LANE), 1)
    work = jnp.where(sq_row == sq_col, 1.0, 0.0) + counts * maps[FUNCS + na + 1, 0]
    other = counts * maps[FUNCS + na, 0]
    row_id = lax.broadcasted_iota(jnp.int32, (na, 1), 0)
    for k in range(na):
        scale = 1.0 / work[k : k + 1, k : k + 1]
        pivot, tail = work[k : k + 1] * scale, other[k : k + 1] * scale
        factor = work[:, k : k + 1]
        work = jnp.where(row_id == k, pivot, work - factor * pivot)
        other = jnp.where(row_id == k, tail, other - factor * tail)
    for k in range(FUNCS):
        plain = maps[k]
        w_func[1, k] = plain
        w_func[0, k] = plain - tree([other[f : f + 1, k : k + 1] * maps[FUNCS + f] for f in range(na)])

    wide = lax.broadcasted_iota(jnp.int32, (nd, na, LANE), 2)
    for c in range(3):
        own = jnp.where(wide == 8 + c, rows, 0.0)
        for k in range(FUNCS):
            base_f[c, k] = jnp.broadcast_to(one(jnp.sum(w_func[min(c, 1), k] * own, axis=0)), (SUB, LANE))

    def finish(slot, h, v0):
        last = scales[SWEEPS - 1]

        def u(x, y):
            return last * h[x + 1, y] + v0[x, y]

        sums = [[], [], [], []]
        for x in range(nx):
            for side, y in ((0, ny - 1), (1, 0)):
                value = u(x, y)
                u_y[slot, side, x] = value
                sums[2 + side].append(value)
        contact = []
        for y in range(ny):
            for side, x in ((0, nx - 1), (1, 0)):
                value = u(x, y)
                u_x[slot, side, y] = value
                sums[side].append(value)
                if side:
                    contact.append(mask[y] * value)
        start_faces(slot)
        normal = jnp.where(lax.rem(slot, 3) == 0, 1.0, 0.0).astype(F32)
        post(slot, [(k, one(tree(s))) for k, s in enumerate(sums)] + [(4, normal * one(tree(contact)))])

    def first(c, carry):
        fs = [base_f[c, k] for k in range(FUNCS)]
        normal = jnp.where(c == 0, 1.0, 0.0).astype(F32)

        source = load.at[c]
        for x, y in face_columns(nx, ny):
            f = zero
            if x == nx - 1:
                f = f + fs[0]
            if x == 0:
                f = f - fs[1] + (normal * fs[4]) * mask[y]
            if y == ny - 1:
                f = f + fs[2]
            if y == 0:
                f = f - fs[3]
            source[x, y] = source[x, y] - q_ref[x, y] * f
        sweep(nx, ny, 1, nx, source, gb.at[c], w_ref, 1.0 / scales[1], source, nx, pad=0)
        bufs = (ga, gb.at[c])
        for k in range(2, SWEEPS):
            sweep(nx, ny, depths[k], nx, bufs[(k - 1) % 2], bufs[k % 2], w_ref, 1.0 / scales[k], source, nx,
                  k == SWEEPS - 1)
        finish(c, bufs[(SWEEPS - 1) % 2], source)
        return carry

    lax.fori_loop(0, 3, first, 0)

    def prepare(slot):
        collect(slot)
        tab, kind = table[slot], jnp.minimum(lax.rem(slot, 3), 1)
        sign = jnp.where(slot < 3, -1.0, 1.0).astype(F32)
        for k in range(FUNCS):
            f_next[k] = jnp.broadcast_to(sign * one(jnp.sum(w_func[kind, k] * tab, axis=0)), (SUB, LANE))

    def project(slot):
        wait_faces(slot)
        c = lax.rem(slot, 3)
        power = lax.div(slot, 3)
        sign = jnp.where(slot < 3, -1.0, 1.0).astype(F32)
        normal = jnp.where(c == 0, 1.0, 0.0).astype(F32)
        fs = [f_next[k] for k in range(FUNCS)]
        field, squares = {}, []

        def add(x, y, value):
            field[x, y] = value if (x, y) not in field else field[x, y] + value

        for y in range(ny):
            head = u_x[slot, 1, y]
            own = sign * (u_x[slot, 0, y] - outer * below_in[slot, y]) - fs[0]
            up = (sign * inner) * (above_in[slot, y] - head) - fs[1]
            touch = normal * mask[y] * (fs[4] - sign * head)
            y_x[slot, 0, y] = own
            y_x[slot, 1, y] = up
            y_c[slot, y] = touch
            squares += [own * own, touch * touch]
            add(nx - 1, y, own)
            add(0, y, -up - touch)
        for x in range(nx):
            own = sign * (u_y[slot, 0, x] - right_in[slot, x]) - fs[2]
            up = sign * (left_in[slot, x] - u_y[slot, 1, x]) - fs[3]
            y_y[slot, 0, x] = own
            y_y[slot, 1, x] = up
            squares.append(own * own)
            add(x, ny - 1, own)
            add(x, 0, -up)
        moments[2 * power] = moments[2 * power] + tree(squares)
        for (x, y), value in field.items():
            f_ref[x, y] = value
            value = q_ref[x, y] * value
            v0[x, y] = value
            la[x + 1, y] = value

    edge = face_columns(nx, ny)

    def krylov(i, carry):
        project(i)
        bufs = (la, lb)
        for k in range(1, SWEEPS):
            if k == SWEEPS - 1:
                prepare(i + 1)
            sweep(nx, ny, min(k, depths[k]), min(k - 1, SWEEPS - 1 - k + 1), bufs[(k - 1) % 2], bufs[k % 2], w_ref,
                  1.0 / scales[k], v0, 0, k == SWEEPS - 1)
        slot = i + 3
        finish(slot, bufs[(SWEEPS - 1) % 2], v0)
        parts = []
        for y in range(ny):
            parts += [y_x[i, 0, y] * u_x[slot, 0, y], -(y_x[i, 1, y] + y_c[i, y]) * u_x[slot, 1, y]]
        for x in range(nx):
            parts += [y_y[i, 0, x] * u_y[slot, 0, x], -y_y[i, 1, x] * u_y[slot, 1, x]]
        odd = 2 * lax.div(i, 3) + 1
        moments[odd] = moments[odd] + tree(parts)
        return carry

    prepare(jnp.int32(0))
    lax.fori_loop(0, 6, krylov, 0)

    def last_moment(i, carry):
        pl.when(i > 6)(lambda: prepare(i))
        project(i)
        sweep(nx, ny, 1, 0, la, lb, w_ref, 1.0 / scales[1], v0, 0)
        sweep(nx, ny, 2, 1, lb, la, w_ref, 1.0 / scales[2], v0, 0)
        square = scales[2] * scales[2]

        acc = [zero]

        def act_on(x, lo, count, center, around):
            acc[0] = acc[0] + jnp.sum((p_ref[x, pl.ds(lo, count)] * center) * (
                (-RELAXATION * square) * center + (KEEP * square) * around), axis=0)

        region(nx, ny, 2, 2, la, w_ref, act_on)
        parts = [f_ref[x, y] * la[x + 1, y] for x, y in edge]
        moments[5] = moments[5] + acc[0] + (2.0 * scales[2]) * tree(parts)
        return carry

    lax.fori_loop(6, 9, last_moment, 0)
    post(SLOTS + 1, [(j, one(moments[j])) for j in range(6)])

    def drain(slot, c):
        faces_sent(slot)
        sent_all(slot)
        return c

    lax.fori_loop(0, SLOTS, drain, 0)
    sent_all(SLOTS)
    collect(SLOTS + 1)
    sums = jnp.sum(jnp.sum(table[SLOTS + 1], axis=0), axis=0, keepdims=True)
    m = [jnp.broadcast_to(sums[:, j : j + 1], (1, LANE)) for j in range(6)]

    a0 = m[0] / m[1]
    g1 = m[0] + 2.0 * a0 * m[1] + a0 * a0 * m[2]
    c1 = 1.0 + g1 / m[0]
    a1 = g1 / (c1 * c1 * m[1] + 2.0 * c1 * a0 * m[2] + a0 * a0 * m[3])
    pp, ss = a0 + a1 * c1, a1 * a0
    g2 = m[0] + 2.0 * pp * m[1] + (pp * pp + 2.0 * ss) * m[2] + 2.0 * pp * ss * m[3] + ss * ss * m[4]
    b2 = g2 / g1
    da, db = 1.0 + b2 * c1, pp + b2 * a0
    a2 = g2 / (da * da * m[1] + 2.0 * da * db * m[2] + (db * db + 2.0 * da * ss) * m[3]
               + 2.0 * db * ss * m[4] + ss * ss * m[5])
    k0 = jnp.broadcast_to(a0 + a1 * c1 + a2 * da, (SUB, LANE))
    k1 = jnp.broadcast_to(a1 * a0 + a2 * db, (SUB, LANE))
    k2 = jnp.broadcast_to(a2 * ss, (SUB, LANE))

    for c in range(3):
        for y in range(ny):
            out_x[c, y] = base_f[c, 0] + (k0 * y_x[c, 0, y] + k1 * y_x[3 + c, 0, y] + k2 * y_x[6 + c, 0, y])
        for x in range(nx):
            out_y[c, x] = base_f[c, 2] + (k0 * y_y[c, 0, x] + k1 * y_y[3 + c, 0, x] + k2 * y_y[6 + c, 0, x])
    for y in range(ny):
        out_c[y] = (k0 * y_c[0, y] + k1 * y_c[3, y] + k2 * y_c[6, y]) - base_f[0, 4] * mask[y]

    sent_all(SLOTS + 1)


def lay_out(in_x, in_y, in_c, out_x, out_y, out_c, sem):
    for zb in range(in_c.shape[1]):
        z = pl.ds(zb * LANE, LANE)
        pltpu.make_async_copy(in_x.at[:, :, zb, :], out_x.at[:, 0, :, z], sem.at[0]).start()
        pltpu.make_async_copy(in_y.at[:, :, zb, :], out_y.at[:, :, 0, z], sem.at[1]).start()
        pltpu.make_async_copy(in_c.at[:, zb, :], out_c.at[0, :, z], sem.at[2]).start()
    for k, ref in enumerate((in_x, in_y, in_c)):
        pltpu.make_async_copy(ref, ref, sem.at[k]).wait()


def shards(external_load, modulus, active):
    nx, ny, nz = modulus.shape
    nd, na = lax.axis_size("body"), lax.axis_size("surf")
    maps = jnp.asarray(coarse_tables(nd, na, float(ny * nz), float(nx * nz)), F32)
    tile = (SUB, LANE)
    padded, grid = (nx + 2, ny) + tile, (nx, ny) + tile
    any_spec = pl.BlockSpec(memory_space=pl.ANY)
    shapes = [
        ((3,) + grid, F32), (grid, F32), ((ny,) + tile, jnp.int32), ((FUNCS + na + 2, nd, na, LANE), F32),
        ((ny,) + tile, F32), (padded, F32), (padded, F32), ((13,) + padded, F32), (grid[:2] + (26,) + tile, F32),
        (grid, F32), (grid, F32)] + [(padded, F32), ((3,) + padded, F32), (padded, F32), (padded, F32)] + [
        (grid, F32), (grid, F32), ((SLOTS, 2, ny) + tile, F32), ((SLOTS, 2, nx) + tile, F32),
        ((SLOTS, ny) + tile, F32), ((SLOTS, ny) + tile, F32), ((SLOTS, nx) + tile, F32), ((SLOTS, nx) + tile, F32),
        ((SLOTS, 2, ny) + tile, F32), ((SLOTS, 2, nx) + tile, F32), ((SLOTS, ny) + tile, F32),
        ((3, FUNCS) + tile, F32), ((FUNCS,) + tile, F32), ((2, FUNCS, nd, na, LANE), F32), ((6,) + tile, F32),
        ((SLOTS + 2,) + tile, F32), ((SLOTS + 2, nd, na, LANE), F32)]
    dma = pltpu.SemaphoreType.DMA
    parts = pl.pallas_call(
        functools.partial(feti_kernel, nx, ny, nz, nd, na),
        out_shape=tuple(jax.ShapeDtypeStruct(s + tile, F32) for s in ((3, ny), (3, nx), (ny,))),
        in_specs=[pl.BlockSpec(memory_space=pltpu.HBM)] * 4, out_specs=(pl.BlockSpec(memory_space=pltpu.VMEM),) * 3,
        scratch_shapes=[pltpu.VMEM(s, t) for s, t in shapes] + [
            dma((6,)), dma((SLOTS, 4)), dma((SLOTS, 4)),
            dma((SLOTS + 2,)), dma((SLOTS + 2,)), dma((SLOTS + 2,))],
        compiler_params=pltpu.CompilerParams(
            vmem_limit_bytes=54700 * 1024, collective_id=0, has_side_effects=True),
    )(external_load, modulus, active, maps)
    return pl.pallas_call(
        lay_out,
        out_shape=(jax.ShapeDtypeStruct((3, 1, ny, nz), F32), jax.ShapeDtypeStruct((3, nx, 1, nz), F32),
                   jax.ShapeDtypeStruct((1, ny, nz), F32)),
        in_specs=[any_spec] * 3, out_specs=(any_spec,) * 3, scratch_shapes=[dma((3,))],
        compiler_params=pltpu.CompilerParams(vmem_limit_bytes=4 * 1024 * 1024),
    )(*parts)


def solution(mesh):
    placed = (P(None, "body", "surf", None), P("body", "surf", None), P("surf", None))
    return jax.shard_map(
        shards,
        mesh=mesh,
        in_specs=placed,
        out_specs=(
            P(None, "body", "surf", None),
            P(None, "body", "surf", None),
            P("body", "surf", None),
        ),
        check_vma=False,
    )
```
